32 devices in a mesh: dp: 4 (over y, core), table: 8 (over z, x).
Axes of the slice: x: 2, y: 2, z: 4, core: 2. Of those that a mesh axis runs over, the one named last changes fastest.
Arguments:
- table: float32 [131072, 256], P(('dp', 'table')), may hold values from -6 to 6
- hidden: float32 [16384, 256], P(('dp', 'table')), may hold values from -24 to 24
- neg_ids: int32 [4, 8, 4, 128], P('dp', 'table'), may hold values from 0 to 4095
- pos_ids: int32 [16384], P(('dp', 'table')), may hold values from 0 to 4095
- dloss: float32 [16384], P(('dp', 'table')), may hold values from -4 to 4
Outputs:
- row_loss: float32 [16384], P(('dp', 'table'))
- grad_hidden: float32 [16384, 256], P(('dp', 'table'))
- grad_table: float32 [131072, 256], P(('dp', 'table'))
The draws below stay inside these ranges and needn't reach their ends.
All inputs are finite; a program needn't handle non-finite values.
Results may differ from the reference program's by a relative error of at most 0.0003.
Values sent between devices are 32-bit elements; how exact they have to be, the bound alone decides.
A program may use at most 192 MiB of HBM per device.

```python
import math
import jax
import jax.numpy as jnp
from jax import lax

D = 256
ROWS_DEV = 4096
NEG_PEER = 128
GROUP_ROWS = 4096
ROWS = 16384
ITEMS = 131072
POOL = 4096
N_DP = 4
N_TABLE = 8


def draw_table(key, part):
    noise_part = jax.random.normal(jax.random.fold_in(key, 21), (ITEMS, D), jnp.float32)
    return jnp.clip(noise_part, -4.0, 4.0)


def draw_hidden(key, part):
    noise_part = jax.random.normal(jax.random.fold_in(key, 31), (ROWS, D), jnp.float32)
    return jnp.clip(noise_part, -4.0, 4.0)


def place_ends(entries, stream_key, least, high):
    longest = entries.shape.index(max(entries.shape))
    spots = []
    for shift in (0, 1):
        where = [jax.random.randint(jax.random.fold_in(stream_key, axis), (), 0, length) for axis, length in enumerate(entries.shape)]
        where[longest] = (where[longest] + shift) % entries.shape[longest]
        spots.append(tuple(where))
    return entries.at[spots[0]].set(least).at[spots[1]].set(high)


def block_scale(key, extent, split, least, high):
    def one(position, parts):
        heights = jax.random.uniform(jax.random.fold_in(jax.random.fold_in(key, 6), position), (parts,), jnp.float32, least / len(split), high / len(split))
        return jnp.repeat(jnp.exp(heights), extent[position] // parts).reshape((-1,) + (1,) * (len(extent) - position - 1))

    level = one(*split[0])
    for cut in split[1:]:
        level = level * one(*cut)
    return level


def centred(own_key, extent, deviation, most, split=(), kind=jnp.bfloat16):
    loudness = block_scale(own_key, extent, split, -0.22, 0.18) if split else 1.0
    drawn = jax.random.normal(own_key, extent, jnp.float32) * deviation * loudness
    return jnp.minimum(jnp.maximum(drawn, -most), most).astype(kind)


def setup_inputs(seed: int = 0) -> dict:
    key_list = jax.random.split(jax.random.key(seed), 6)
    return {
        "table": draw_table(jax.random.fold_in(key_list[5], 71), 0),
        "hidden": draw_hidden(jax.random.fold_in(key_list[5], 71), 0),
        "neg_ids": place_ends(jax.random.randint(key_list[2], (N_DP, N_TABLE, N_DP, NEG_PEER), 0, ROWS_DEV), jax.random.fold_in(key_list[2], 1), 0, ROWS_DEV - 1).astype(jnp.int32),
        "pos_ids": place_ends(jax.random.randint(key_list[3], (ROWS,), 0, POOL), jax.random.fold_in(key_list[3], 1), 0, POOL - 1).astype(jnp.int32),
        "dloss": centred(key_list[4], (ROWS,), 1.0, 4.0, ((0, 32),), jnp.float32),
    }


def reference(table, hidden, neg_ids, pos_ids, dloss):
    logit_scale = 3.0 / math.sqrt(D)
    owners = (jnp.arange(N_DP, dtype=jnp.int32)[:, None] * N_TABLE + jnp.arange(N_TABLE, dtype=jnp.int32)[None, :]).astype(jnp.int32)
    grad_table = jnp.zeros(table.shape, jnp.float32)
    loss_list = []
    grad_list = []
    for group_index in range(N_DP):
        local_ids = neg_ids[:, :, group_index, :]
        global_rows = owners[:, :, None] * ROWS_DEV + local_ids
        global_rows = jnp.transpose(global_rows, (1, 0, 2)).reshape(-1).astype(jnp.int32)
        candidates = table[global_rows]
        group_hidden = hidden[group_index * GROUP_ROWS:(group_index + 1) * GROUP_ROWS]
        targets = pos_ids[group_index * GROUP_ROWS:(group_index + 1) * GROUP_ROWS]
        weights = dloss[group_index * GROUP_ROWS:(group_index + 1) * GROUP_ROWS]
        logits = logit_scale * lax.dot_general(group_hidden, candidates, (((1,), (1,)), ((), ())), precision=lax.Precision.HIGHEST, preferred_element_type=jnp.float32)
        row_max = lax.optimization_barrier(jnp.max(logits, axis=1))
        exponent = jnp.exp(logits - row_max[:, None])
        row_total = lax.optimization_barrier(jnp.sum(exponent, axis=1))
        onehot = (jnp.arange(POOL, dtype=jnp.int32)[None, :] == targets[:, None]).astype(jnp.float32)
        target_logit = lax.optimization_barrier(jnp.sum(logits * onehot, axis=1))
        loss_list.append(row_max + jnp.log(row_total) - target_logit)
        coefficient = logit_scale * weights[:, None] * (exponent / row_total[:, None] - onehot)
        grad_list.append(jnp.dot(coefficient, candidates, precision=lax.Precision.HIGHEST, preferred_element_type=jnp.float32))
        cand_grad = lax.dot_general(coefficient, group_hidden, (((0,), (0,)), ((), ())), precision=lax.Precision.HIGHEST, preferred_element_type=jnp.float32)
        grad_table = grad_table.at[global_rows].add(cand_grad)
    return (jnp.concatenate(loss_list), jnp.concatenate(grad_list, axis=0), grad_table)
```

```python
import functools
import math

import jax
import jax.numpy as jnp
from jax import lax
from jax.experimental import pallas as pl
from jax.experimental.pallas import tpu as pltpu
from jax.sharding import PartitionSpec as P

MESH = pl.DeviceIdType.MESH


def split(x):
    high = x.astype(jnp.bfloat16)
    return high, (x - high.astype(jnp.float32)).astype(jnp.bfloat16)


def kernel(
    peers, near, scale,
    out_ref, hid_ref, side_ref,
    loss_ref, gh_ref, back_ref,
    cand, ct_hi, ct_lo, hid, h_hi, h_lo, side, expo, bstat, stat, aim, lossbuf, merged, cg, ret, ght, ghmate, ghrecv,
    c_send, c_recv, h_send, h_recv, m_send, m_recv, d_send, d_recv, e_send, e_recv,
    t_send, t_recv, a_send, a_recv, l_send, l_recv, z_send, z_recv, x_send, x_recv, g_send, g_recv,
):
    me = lax.axis_index("dp")
    t = lax.axis_index("table")
    a, k = me // 2, lax.rem(me, 2)
    hi, lo, s = t // (near * 2), lax.rem(t // 2, near), lax.rem(t, 2)
    rows, width = hid_ref.shape
    per = out_ref.shape[1]
    halves = peers // 2
    count = peers * per
    piece = 2 * per
    blocks = 2 * near
    mine = a * 2 + s
    same = s == k
    other = 1 - k

    def place(far, mid, last):
        return far * (near * 2) + mid * 2 + last

    def wrap(base, step, size):
        return lax.rem(base + step, size)

    def device(da, dk, dh, dl, ds):
        return (
            wrap(a, da, halves) * 2 + wrap(k, dk, 2),
            place(wrap(hi, dh, 2), wrap(lo, dl, near), wrap(s, ds, 2)),
        )

    both = (0, 1)
    greet = [
        (da, dk, dh, dl, ds)
        for da in range(halves) for dk in both for dh in both for dl in range(near) for ds in both
        if (da, dk, dh, dl, ds) != (0, 0, 0, 0, 0) and (dl == 0 or (da == 0 and dh == 0))
    ]
    barrier = pltpu.get_barrier_semaphore()
    for g in greet:
        pl.semaphore_signal(barrier, inc=1, device_id=device(*g), device_id_type=MESH)
    pl.semaphore_wait(barrier, len(greet))

    started = []

    def send(src, dst, ssem, rsem, dev, own=None):
        copy = pltpu.make_async_remote_copy(
            src_ref=src, dst_ref=dst, send_sem=ssem, recv_sem=rsem, device_id=dev, device_id_type=MESH
        )
        if own is None:
            copy.start()
        else:
            @pl.when(own)
            def _():
                pltpu.make_async_copy(src, dst, rsem).start()

            @pl.when(jnp.logical_not(own))
            def _():
                copy.start()
        started.append((copy, own))

    def arrive(dst, rsem):
        pltpu.make_async_copy(dst, dst, rsem).wait()

    def send_cand(dh, da, dc):
        to = wrap(a, da, halves)
        g = to * 2 + wrap(s, dc, 2)
        send(
            out_ref.at[g], cand.at[dh, me], c_send.at[dh, g], c_recv.at[dh, me],
            (to * 2 + s, place(wrap(hi, dh, 2), lo, wrap(s, dc, 2))),
            same if (dh, da, dc) == (0, 0, 0) else None,
        )

    def send_hid(dl):
        dev = (mine, place(hi, wrap(lo, dl, near), k))
        own = same if dl == 0 else None
        send(side_ref, side.at[s, lo], d_send.at[dl], d_recv.at[lo], dev, own)
        send(hid_ref, hid.at[s, lo], h_send.at[dl], h_recv.at[lo], dev, own)

    for da in range(halves - 1, -1, -1):
        for dc in both:
            send_cand(1, da, dc)
    for dl in range(1, near):
        send_hid(dl)
    send_hid(0)
    for da in range(halves):
        for dc in both:
            send_cand(0, da, dc)

    mate = (a * 2 + other, t)

    def take_hid(dl):
        mid = wrap(lo, dl, near)
        arrive(side.at[k, mid], d_recv.at[mid])
        arrive(hid.at[k, mid], h_recv.at[mid])
        send(side.at[k, mid], side.at[k, mid], e_send.at[mid], e_recv.at[mid], mate)
        send(hid.at[k, mid], hid.at[k, mid], m_send.at[mid], m_recv.at[mid], mate)
        cut(k, mid)

    def take_mate(dl):
        mid = wrap(lo, dl, near)
        arrive(side.at[other, mid], e_recv.at[mid])
        arrive(hid.at[other, mid], m_recv.at[mid])
        cut(other, mid)

    def cut(x, mid):
        top, low = split(hid[x, mid])
        h_hi[x, mid] = top
        h_lo[x, mid] = low

    def hits(dh, j, x, mid):
        base = place(wrap(hi, dh, 2), lo, k) * count + wrap(a, j, halves) * piece
        index = lax.broadcasted_iota(jnp.int32, (piece, rows), 0) + base
        return index == side[x, mid, 0:1, :].astype(jnp.int32)

    def take_cand(dh, j):
        for dk in both:
            source = wrap(a, j, halves) * 2 + wrap(k, dk, 2)
            arrive(cand.at[dh, source], c_recv.at[dh, source])

    def forward(dh, j, first, last):
        block = cand[dh, pl.ds(wrap(a, j, halves) * 2, 2)].reshape(piece, width)
        b_hi, b_lo = split(block)
        if first == 0:
            turned = split(block.T)
            ct_hi[dh, j] = turned[0]
            ct_lo[dh, j] = turned[1]
        left = jnp.concatenate([b_hi, b_lo, b_hi], axis=1)

        def step(i, carry):
            x, mid = lax.rem(i, 2), wrap(lo, i // 2, near)
            right = jnp.concatenate([h_hi[x, mid], h_hi[x, mid], h_lo[x, mid]], axis=1)
            logits = scale * lax.dot_general(
                left, right, (((1,), (1,)), ((), ())), preferred_element_type=jnp.float32
            )
            peak = jnp.max(logits, axis=0, keepdims=True)
            power = jnp.exp(logits - peak)
            expo[dh, j, x, mid] = power
            bstat[dh, j, x, mid, 0:1, :] = peak
            bstat[dh, j, x, mid, 1:2, :] = jnp.sum(power, axis=0, keepdims=True)
            bstat[dh, j, x, mid, 2:3, :] = jnp.sum(
                jnp.where(hits(dh, j, x, mid), logits, 0.0), axis=0, keepdims=True
            )
            return carry

        lax.fori_loop(first, last, step, 0)

    take_hid(0)
    take_mate(0)
    for j in range(halves):
        take_cand(0, j)
        forward(0, j, 0, 2)
    for dl in range(1, near):
        take_hid(dl)
    for dl in range(1, near):
        take_mate(dl)
    for j in range(halves):
        forward(0, j, 2, blocks)
    for j in range(halves - 1, -1, -1):
        take_cand(1, j)
        forward(1, j, 0, blocks)

    parts = [(dh, j) for dh in both for j in range(halves)]
    seat = k * near + lo
    for x in both:
        for mid in range(near):
            m = x * near + mid
            peak = bstat[0, 0, x, mid, 0:1, :]
            for p in parts[1:]:
                peak = jnp.maximum(peak, bstat[p[0], p[1], x, mid, 0:1, :])
            total = jnp.zeros_like(peak)
            target = jnp.zeros_like(peak)
            for p in parts:
                total += bstat[p[0], p[1], x, mid, 1:2, :] * jnp.exp(bstat[p[0], p[1], x, mid, 0:1, :] - peak)
                target += bstat[p[0], p[1], x, mid, 2:3, :]
            stat[seat, m : m + 1, :] = peak
            stat[seat, blocks + m : blocks + m + 1, :] = total
            aim[seat, m : m + 1, :] = target
    crew = [(dk, dl) for dl in range(near - 1, -1, -1) for dk in both if (dk, dl) != (0, 0)]
    for dk, dl in crew:
        send(
            stat.at[seat], stat.at[seat], t_send.at[dk, dl], t_recv.at[dk, dl], device(0, dk, 0, dl, 0)
        )
    for dk, dl in crew:
        send(
            aim.at[seat], aim.at[seat], a_send.at[dk, dl], a_recv.at[dk, dl], device(0, dk, 0, dl, 0)
        )
    for dk, dl in crew:
        came = wrap(k, dk, 2) * near + wrap(lo, near - dl, near)
        arrive(stat.at[came], t_recv.at[dk, dl])

    for x in both:
        for mid in range(near):
            m = x * near + mid
            peak = stat[0, m : m + 1, :]
            for w in range(1, blocks):
                peak = jnp.maximum(peak, stat[w, m : m + 1, :])
            total = jnp.zeros_like(peak)
            for w in range(blocks):
                total += stat[w, blocks + m : blocks + m + 1, :] * jnp.exp(stat[w, m : m + 1, :] - peak)
            weight = scale * side[x, mid, 1:2, :]
            merged[x, mid, 0:1, :] = peak
            merged[x, mid, 1:2, :] = weight / total
            merged[x, mid, 2:3, :] = weight
            merged[x, mid, 3:4, :] = peak + jnp.log(total)

    ght[...] = jnp.zeros_like(ght)

    def backward(dh, j):
        flip = jnp.concatenate([ct_hi[dh, j], ct_hi[dh, j], ct_lo[dh, j]], axis=1)

        def step(i, acc):
            x, mid = lax.rem(i, 2), i // 2
            weight = merged[x, mid, 2:3, :]
            factor = merged[x, mid, 1:2, :] * jnp.exp(bstat[dh, j, x, mid, 0:1, :] - merged[x, mid, 0:1, :])
            power = expo[dh, j, x, mid] * factor
            c_hi, c_lo = split(jnp.where(hits(dh, j, x, mid), power - weight, power))
            ght[x, mid] += jnp.dot(
                flip, jnp.concatenate([c_hi, c_lo, c_hi], axis=0), preferred_element_type=jnp.float32
            )
            return acc + jnp.dot(
                jnp.concatenate([c_hi, c_lo, c_hi], axis=1),
                jnp.concatenate([h_hi[x, mid], h_hi[x, mid], h_lo[x, mid]], axis=0),
                preferred_element_type=jnp.float32,
            )

        acc = lax.fori_loop(0, blocks, step, jnp.zeros((piece, width), jnp.float32))
        start = wrap(a, j, halves) * 2
        cg[dh, pl.ds(start, 2)] = acc.reshape(2, per, width)
        for dk in both:
            source = start + wrap(k, dk, 2)
            send(
                cg.at[dh, source], ret.at[dh, mine], z_send.at[dh, source], z_recv.at[dh, mine],
                (source, place(wrap(hi, dh, 2), lo, k)),
                same if (dh, j, dk) == (0, 0, 0) else None,
            )

    for dh in (1, 0):
        for j in range(halves - 1, -1, -1):
            backward(dh, j)

    for dl in range(near - 1, -1, -1):
        mid = wrap(lo, dl, near)
        send(ght.at[other, mid], ghmate.at[mid], x_send.at[mid], x_recv.at[mid], mate)
    for dl in range(near - 1, -1, -1):
        mid = wrap(lo, dl, near)
        arrive(ghmate.at[mid], x_recv.at[mid])
        ght[k, mid] += ghmate[mid]
        send(
            ght.at[k, mid], ghrecv.at[lo], g_send.at[dl], g_recv.at[lo],
            (mine, place(hi, mid, k)), same if dl == 0 else None,
        )

    for dk, dl in crew:
        came = wrap(k, dk, 2) * near + wrap(lo, near - dl, near)
        arrive(aim.at[came], a_recv.at[dk, dl])
    target = jnp.zeros((1, rows), jnp.float32)
    for w in range(blocks):
        target += aim[w, pl.ds(seat, 1), :]
    lossbuf[0] = jnp.broadcast_to(merged[k, lo, 3:4, :] - target, lossbuf.shape[1:])
    send(lossbuf.at[0], lossbuf.at[1], l_send, l_recv, (mine, place(hi, lo, k)), same)

    for dl in range(near):
        mid = wrap(lo, dl, near)
        arrive(ghrecv.at[mid], g_recv.at[mid])
    whole = ghrecv[0]
    for mid in range(1, near):
        whole += ghrecv[mid]
    gh_ref[...] = whole.T
    arrive(lossbuf.at[1], l_recv)
    loss_ref[...] = lossbuf[1, 0:1, :]
    for dh in both:
        for g in range(peers):
            arrive(ret.at[dh, g], z_recv.at[dh, g])
    back_ref[...] = ret[0] + ret[1]
    for copy, own in started:
        if own is None:
            copy.wait_send()
        else:
            @pl.when(jnp.logical_not(own))
            def _():
                copy.wait_send()


def local(table, hidden, neg_ids, pos_ids, dloss):
    rows, width = hidden.shape
    scale = 3.0 / math.sqrt(width)
    peers = lax.axis_size("dp")
    near = lax.axis_size("table") // 4
    flat_ids = neg_ids[0, 0].reshape(-1)
    per = neg_ids.shape[3]
    count = peers * per
    halves, blocks, piece = peers // 2, 2 * near, 2 * per
    outgoing = table.at[flat_ids].get(mode="promise_in_bounds").reshape(peers, per, width)
    side = jnp.stack([pos_ids.astype(jnp.float32), dloss] + [dloss] * 6, axis=0)
    f32, bf16 = jnp.float32, jnp.bfloat16
    pairs = pltpu.SemaphoreType.DMA((2, peers))
    nears = pltpu.SemaphoreType.DMA((near,))
    crews = pltpu.SemaphoreType.DMA((2, near))
    vmem = pl.BlockSpec(memory_space=pltpu.VMEM)
    flops = 18 * 4 * count * near * rows * width
    loss, grad_hidden, returned = pl.pallas_call(
        functools.partial(kernel, peers, near, scale),
        out_shape=(
            jax.ShapeDtypeStruct((1, rows), f32),
            jax.ShapeDtypeStruct((rows, width), f32),
            jax.ShapeDtypeStruct((peers, per, width), f32),
        ),
        in_specs=[vmem] * 3,
        out_specs=(vmem,) * 3,
        scratch_shapes=[
            pltpu.VMEM((2, peers, per, width), f32),
            pltpu.VMEM((2, halves, width, piece), bf16),
            pltpu.VMEM((2, halves, width, piece), bf16),
            pltpu.VMEM((2, near, rows, width), f32),
            pltpu.VMEM((2, near, rows, width), bf16),
            pltpu.VMEM((2, near, rows, width), bf16),
            pltpu.VMEM((2, near, 8, rows), f32),
            pltpu.VMEM((2, halves, 2, near, piece, rows), f32),
            pltpu.VMEM((2, halves, 2, near, 8, rows), f32),
            pltpu.VMEM((blocks, 2 * blocks, rows), f32),
            pltpu.VMEM((blocks, max(8, blocks), rows), f32),
            pltpu.VMEM((2, 8, rows), f32),
            pltpu.VMEM((2, near, 8, rows), f32),
            pltpu.VMEM((2, peers, per, width), f32),
            pltpu.VMEM((2, peers, per, width), f32),
            pltpu.VMEM((2, near, width, rows), f32),
            pltpu.VMEM((near, width, rows), f32),
            pltpu.VMEM((near, width, rows), f32),
            pairs, pairs, nears, nears, nears, nears, nears, nears, nears, nears,
            crews, crews, crews, crews, pltpu.SemaphoreType.DMA, pltpu.SemaphoreType.DMA,
            pairs, pairs, nears, nears, nears, nears,
        ],
        compiler_params=pltpu.CompilerParams(
            collective_id=0, has_side_effects=True, vmem_limit_bytes=67043328
        ),
        cost_estimate=pl.CostEstimate(flops=flops, bytes_accessed=4 * count * width, transcendentals=0),
    )(outgoing, hidden, side)
    grad_table = (
        jnp.zeros(table.shape, f32)
        .at[flat_ids]
        .add(returned.reshape(count, width), mode="promise_in_bounds")
    )
    return (loss.reshape(rows), grad_hidden, grad_table)


def solution(mesh):
    in_specs = (
        P(("dp", "table"), None),
        P(("dp", "table"), None),
        P("dp", "table", None, None),
        P(("dp", "table")),
        P(("dp", "table")),
    )
    out_specs = (P(("dp", "table")), P(("dp", "table"), None), P(("dp", "table"), None))
    return jax.shard_map(local, mesh=mesh, in_specs=in_specs, out_specs=out_specs, check_vma=False)
```

```python
import functools
import math

import jax
import jax.numpy as jnp
from jax import lax
from jax.experimental import pallas as pl
from jax.experimental.pallas import tpu as pltpu
from jax.sharding import PartitionSpec as P

MESH = pl.DeviceIdType.MESH


def split(x):
    high = x.astype(jnp.bfloat16)
    return high, (x - high.astype(jnp.float32)).astype(jnp.bfloat16)


def kernel(
    peers, near, scale,
    ids_ref, pos_ref, dloss_ref, hid_ref, table_ref,
    loss_ref, gh_ref, back_ref,
    out, note, cand, ct_hi, ct_lo, hid, h_hi, h_lo, side, expo, bstat, stat, aim, lossbuf, merged, cg, ret, ght, ghmate, ghrecv,
    table_sem, c_send, c_recv, h_send, h_recv, m_send, m_recv, d_send, d_recv, e_send, e_recv,
    t_send, t_recv, a_send, a_recv, l_send, l_recv, z_send, z_recv, x_send, x_recv, g_send, g_recv,
):
    me = lax.axis_index("dp")
    t = lax.axis_index("table")
    a, k = me // 2, lax.rem(me, 2)
    hi, lo, s = t // (near * 2), lax.rem(t // 2, near), lax.rem(t, 2)
    rows, width = hid_ref.shape
    per = ids_ref.shape[1]
    halves = peers // 2
    count = peers * per
    piece = 2 * per
    blocks = 2 * near
    mine = a * 2 + s
    same = s == k
    other = 1 - k
    ln2 = math.log(2.0)
    bend = scale / ln2

    def place(far, mid, last):
        return far * (near * 2) + mid * 2 + last

    def wrap(base, step, size):
        return lax.rem(base + step, size)

    def device(da, dk, dh, dl, ds):
        return (
            wrap(a, da, halves) * 2 + wrap(k, dk, 2),
            place(wrap(hi, dh, 2), wrap(lo, dl, near), wrap(s, ds, 2)),
        )

    items = table_ref.shape[0]
    bring = pltpu.make_async_copy(table_ref, expo.at[pl.ds(0, items)], table_sem)
    bring.start()
    both = (0, 1)
    greet = [
        (da, dk, dh, dl, ds)
        for da in range(halves) for dk in both for dh in both for dl in range(near) for ds in both
        if (da, dk, dh, dl, ds) != (0, 0, 0, 0, 0) and (dl == 0 or (da == 0 and dh == 0))
    ]
    barrier = pltpu.get_barrier_semaphore()
    for g in greet:
        pl.semaphore_signal(barrier, inc=1, device_id=device(*g), device_id_type=MESH)
    note[0:1, :] = pos_ref[...].astype(jnp.float32)
    note[1:2, :] = dloss_ref[...]
    bring.wait()

    def pick(da, dc):
        g = wrap(a, da, halves) * 2 + wrap(s, dc, 2)

        def row(i, carry):
            out[g, pl.ds(i, 1), :] = expo[pl.ds(ids_ref[g, i], 1), :]
            return carry

        lax.fori_loop(0, per, row, 0, unroll=8)

    for da in range(halves - 1, -1, -1):
        for dc in both:
            pick(da, dc)
    pl.semaphore_wait(barrier, len(greet))

    started = []

    def send(src, dst, ssem, rsem, dev, own=None):
        copy = pltpu.make_async_remote_copy(
            src_ref=src, dst_ref=dst, send_sem=ssem, recv_sem=rsem, device_id=dev, device_id_type=MESH
        )
        if own is None:
            copy.start()
        else:
            @pl.when(own)
            def _():
                pltpu.make_async_copy(src, dst, rsem).start()

            @pl.when(jnp.logical_not(own))
            def _():
                copy.start()
        started.append((copy, own))

    def arrive(dst, rsem):
        pltpu.make_async_copy(dst, dst, rsem).wait()

    def send_cand(dh, da, dc):
        to = wrap(a, da, halves)
        g = to * 2 + wrap(s, dc, 2)
        send(
            out.at[g], cand.at[dh, me], c_send.at[dh, g], c_recv.at[dh, me],
            (to * 2 + s, place(wrap(hi, dh, 2), lo, wrap(s, dc, 2))),
            same if (dh, da, dc) == (0, 0, 0) else None,
        )

    def send_hid(dl):
        dev = (mine, place(hi, wrap(lo, dl, near), k))
        own = same if dl == 0 else None
        send(note, side.at[s, lo], d_send.at[dl], d_recv.at[lo], dev, own)
        send(hid_ref, hid.at[s, lo], h_send.at[dl], h_recv.at[lo], dev, own)

    later = range(1, near)
    far = range(halves - 1, -1, -1)
    SENDS = [("c", 1, da, dc) for da in far for dc in both]
    SENDS += [("h", dl) for dl in later] + [("h", 0)]
    SENDS += [("c", 0, da, dc) for da in range(halves) for dc in both]
    for item in SENDS:
        if item[0] == "c":
            send_cand(*item[1:])
        else:
            send_hid(item[1])

    mate = (a * 2 + other, t)

    def take_hid(dl):
        mid = wrap(lo, dl, near)
        arrive(side.at[k, mid], d_recv.at[mid])
        arrive(hid.at[k, mid], h_recv.at[mid])
        send(side.at[k, mid], side.at[k, mid], e_send.at[mid], e_recv.at[mid], mate)
        send(hid.at[k, mid], hid.at[k, mid], m_send.at[mid], m_recv.at[mid], mate)
        cut(k, mid)

    def take_mate(dl):
        mid = wrap(lo, dl, near)
        arrive(side.at[other, mid], e_recv.at[mid])
        arrive(hid.at[other, mid], m_recv.at[mid])
        cut(other, mid)

    def cut(x, mid):
        top, low = split(hid[x, mid] * bend)
        h_hi[x, mid] = top
        h_lo[x, mid] = low

    def hits(dh, j, x, mid):
        base = place(wrap(hi, dh, 2), lo, k) * count + wrap(a, j, halves) * piece
        index = lax.broadcasted_iota(jnp.int32, (piece, rows), 0) + base
        return index == side[x, mid, 0:1, :].astype(jnp.int32)

    def take_cand(dh, j):
        for dk in both:
            source = wrap(a, j, halves) * 2 + wrap(k, dk, 2)
            arrive(cand.at[dh, source], c_recv.at[dh, source])

    folds = rows // width

    def slot(dh, j, x, mid, fold):
        first = ((((dh * halves + j) * 2 + x) * near + mid) * folds + fold) * piece
        return pl.ds(pl.multiple_of(first, piece), piece)

    def keep(dh, j, x, mid, value):
        for fold in range(folds):
            expo[slot(dh, j, x, mid, fold), :] = value[:, fold * width : (fold + 1) * width]

    def kept(dh, j, x, mid):
        return jnp.concatenate([expo[slot(dh, j, x, mid, fold), :] for fold in range(folds)], axis=1)

    def turn(dh, j):
        turned = split(cand[dh, pl.ds(wrap(a, j, halves) * 2, 2)].reshape(piece, width).T)
        ct_hi[dh, j] = turned[0]
        ct_lo[dh, j] = turned[1]

    def forward(dh, j, first, last):
        block = cand[dh, pl.ds(wrap(a, j, halves) * 2, 2)].reshape(piece, width)
        b_hi, b_lo = split(block)
        left = jnp.concatenate([b_hi, b_lo, b_hi], axis=1)

        def step(i, carry):
            x, mid = lax.rem(i, 2), wrap(lo, i // 2, near)
            right = jnp.concatenate([h_hi[x, mid], h_hi[x, mid], h_lo[x, mid]], axis=1)
            logits = lax.dot_general(
                left, right, (((1,), (1,)), ((), ())), preferred_element_type=jnp.float32
            )
            peak = jnp.max(logits, axis=0, keepdims=True)
            power = jnp.exp2(logits - peak)
            keep(dh, j, x, mid, power)
            bstat[dh, j, x, mid, 0:1, :] = peak
            bstat[dh, j, x, mid, 1:2, :] = jnp.sum(power, axis=0, keepdims=True)
            bstat[dh, j, x, mid, 2:3, :] = jnp.sum(
                jnp.where(hits(dh, j, x, mid), logits, 0.0), axis=0, keepdims=True
            )
            return carry

        lax.fori_loop(first, last, step, 0, unroll=2)

    STEPS = [(take_hid, 0), (take_mate, 0)]
    for j in range(halves):
        STEPS += [(take_cand, 0, j), (forward, 0, j, 0, 2), (turn, 0, j)]
    STEPS += [(take_cand, 1, far[0]), (forward, 1, far[0], 0, 2), (turn, 1, far[0])]
    STEPS += [(take_hid, dl) for dl in later] + [(take_mate, dl) for dl in later]
    STEPS += [(forward, 0, j, 2, blocks) for j in range(halves)]
    STEPS += [(forward, 1, far[0], 2, blocks)]
    for j in far[1:]:
        STEPS += [(take_cand, 1, j), (forward, 1, j, 0, blocks), (turn, 1, j)]
    for todo in STEPS:
        todo[0](*todo[1:])

    parts = [(dh, j) for dh in both for j in range(halves)]
    seat = k * near + lo
    for x in both:
        for mid in range(near):
            m = x * near + mid
            peak = bstat[0, 0, x, mid, 0:1, :]
            for p in parts[1:]:
                peak = jnp.maximum(peak, bstat[p[0], p[1], x, mid, 0:1, :])
            total = jnp.zeros_like(peak)
            target = jnp.zeros_like(peak)
            for p in parts:
                total += bstat[p[0], p[1], x, mid, 1:2, :] * jnp.exp2(bstat[p[0], p[1], x, mid, 0:1, :] - peak)
                target += bstat[p[0], p[1], x, mid, 2:3, :]
            stat[seat, m : m + 1, :] = peak
            stat[seat, blocks + m : blocks + m + 1, :] = total
            aim[seat, m : m + 1, :] = target
    crew = [(dk, dl) for dl in range(near - 1, -1, -1) for dk in both if (dk, dl) != (0, 0)]
    for dk, dl in crew:
        send(
            stat.at[seat], stat.at[seat], t_send.at[dk, dl], t_recv.at[dk, dl], device(0, dk, 0, dl, 0)
        )
    for dk, dl in crew:
        send(
            aim.at[seat], aim.at[seat], a_send.at[dk, dl], a_recv.at[dk, dl], device(0, dk, 0, dl, 0)
        )
    for dk, dl in crew:
        came = wrap(k, dk, 2) * near + wrap(lo, near - dl, near)
        arrive(stat.at[came], t_recv.at[dk, dl])

    for x in both:
        for mid in range(near):
            m = x * near + mid
            peak = stat[0, m : m + 1, :]
            for w in range(1, blocks):
                peak = jnp.maximum(peak, stat[w, m : m + 1, :])
            total = jnp.zeros_like(peak)
            for w in range(blocks):
                total += stat[w, blocks + m : blocks + m + 1, :] * jnp.exp2(stat[w, m : m + 1, :] - peak)
            weight = ln2 * side[x, mid, 1:2, :]
            merged[x, mid, 0:1, :] = peak
            merged[x, mid, 1:2, :] = weight / total
            merged[x, mid, 2:3, :] = weight
            merged[x, mid, 3:4, :] = ln2 * peak + jnp.log(total)

    def backward(dh, j, first, last, fresh):
        flip = jnp.concatenate([ct_hi[dh, j], ct_hi[dh, j], ct_lo[dh, j]], axis=1)

        def step(i, acc):
            x, mid = lax.rem(i, 2), wrap(lo, i // 2, near)
            weight = merged[x, mid, 2:3, :]
            factor = merged[x, mid, 1:2, :] * jnp.exp2(bstat[dh, j, x, mid, 0:1, :] - merged[x, mid, 0:1, :])
            power = kept(dh, j, x, mid) * factor
            c_hi, c_lo = split(jnp.where(hits(dh, j, x, mid), power - weight, power))
            term = jnp.dot(
                flip, jnp.concatenate([c_hi, c_lo, c_hi], axis=0), preferred_element_type=jnp.float32
            )
            if fresh:
                ght[x, mid] = term
            else:
                ght[x, mid] += term
            return acc + jnp.dot(
                jnp.concatenate([c_hi, c_lo, c_hi], axis=1),
                jnp.concatenate([h_hi[x, mid], h_hi[x, mid], h_lo[x, mid]], axis=0),
                preferred_element_type=jnp.float32,
            )

        start = wrap(a, j, halves) * 2
        if last == blocks:
            acc = jnp.zeros((piece, width), jnp.float32)
        else:
            acc = cg[dh, pl.ds(start, 2)].reshape(piece, width)
        acc = lax.fori_loop(first, last, step, acc, unroll=2)
        cg[dh, pl.ds(start, 2)] = acc.reshape(2, per, width)

    def send_back(dh, j):
        start = wrap(a, j, halves) * 2
        for dk in both:
            source = start + wrap(k, dk, 2)
            send(
                cg.at[dh, source], ret.at[dh, mine], z_send.at[dh, source], z_recv.at[dh, mine],
                (source, place(wrap(hi, dh, 2), lo, k)),
                same if (dh, j, dk) == (0, 0, 0) else None,
            )

    def pass_hid(dl):
        mid = wrap(lo, dl, near)
        send(ght.at[other, mid], ghmate.at[mid], x_send.at[mid], x_recv.at[mid], mate)

    def sum_hid(dl):
        mid = wrap(lo, dl, near)
        arrive(ghmate.at[mid], x_recv.at[mid])
        ght[k, mid] += ghmate[mid]
        send(
            ght.at[k, mid], ghrecv.at[lo], g_send.at[dl], g_recv.at[lo],
            (mine, place(hi, mid, k)), same if dl == 0 else None,
        )

    order = [(1, j) for j in far] + [(0, j) for j in far]
    head, tail = order[0], order[1:]
    STEPS = [(backward, *head, 0, blocks, True), (send_back, *head)]
    STEPS += [(backward, *p, 2, blocks, False) for p in tail]
    STEPS += [(pass_hid, dl) for dl in later]
    STEPS += [(backward, *tail[0], 0, 2, False), (send_back, *tail[0])]
    STEPS += [(sum_hid, dl) for dl in later]
    for p in tail[1:]:
        STEPS += [(backward, *p, 0, 2, False), (send_back, *p)]
    STEPS += [(pass_hid, 0), (sum_hid, 0)]
    for todo in STEPS:
        todo[0](*todo[1:])

    for dk, dl in crew:
        came = wrap(k, dk, 2) * near + wrap(lo, near - dl, near)
        arrive(aim.at[came], a_recv.at[dk, dl])
    target = jnp.zeros((1, rows), jnp.float32)
    for w in range(blocks):
        target += aim[w, pl.ds(seat, 1), :]
    lossbuf[0] = jnp.broadcast_to(merged[k, lo, 3:4, :] - ln2 * target, lossbuf.shape[1:])
    send(lossbuf.at[0], lossbuf.at[1], l_send, l_recv, (mine, place(hi, lo, k)), same)

    for dl in range(near):
        mid = wrap(lo, dl, near)
        arrive(ghrecv.at[mid], g_recv.at[mid])
    whole = ghrecv[0]
    for mid in range(1, near):
        whole += ghrecv[mid]
    gh_ref[...] = (bend * whole).T
    arrive(lossbuf.at[1], l_recv)
    loss_ref[...] = lossbuf[1, 0:1, :]
    for dh in both:
        for g in range(peers):
            arrive(ret.at[dh, g], z_recv.at[dh, g])
    back_ref[...] = ret[0] + ret[1]
    for copy, own in started:
        if own is None:
            copy.wait_send()
        else:
            @pl.when(jnp.logical_not(own))
            def _():
                copy.wait_send()


def scatter(ids_ref, loss_in, gh_in, back_ref, loss_ref, gh_ref, out_ref, parts):
    step = pl.program_id(0)
    chunk, count = out_ref.shape[0], ids_ref.shape[1]

    @pl.when(step == 0)
    def _():
        loss_ref[...] = loss_in[...]
        gh_ref[...] = gh_in[...]
        top, low = split(back_ref[...])
        parts[:count] = top
        parts[count:] = low

    index = lax.broadcasted_iota(jnp.int32, (chunk, count), 0) + step * chunk
    chosen = (index == ids_ref[...]).astype(jnp.bfloat16)
    out_ref[...] = jnp.dot(
        jnp.concatenate([chosen, chosen], axis=1), parts[...], preferred_element_type=jnp.float32
    )


def local(table, hidden, neg_ids, pos_ids, dloss):
    rows, width = hidden.shape
    scale = 3.0 / math.sqrt(width)
    peers = lax.axis_size("dp")
    near = lax.axis_size("table") // 4
    ids = neg_ids[0, 0]
    per = neg_ids.shape[3]
    count = peers * per
    halves, blocks, piece = peers // 2, 2 * near, 2 * per
    f32, bf16 = jnp.float32, jnp.bfloat16
    pairs = pltpu.SemaphoreType.DMA((2, peers))
    nears = pltpu.SemaphoreType.DMA((near,))
    crews = pltpu.SemaphoreType.DMA((2, near))
    vmem = pl.BlockSpec(memory_space=pltpu.VMEM)
    flops = 18 * 4 * count * near * rows * width
    loss, grad_hidden, returned = pl.pallas_call(
        functools.partial(kernel, peers, near, scale),
        out_shape=(
            jax.ShapeDtypeStruct((1, rows), f32),
            jax.ShapeDtypeStruct((rows, width), f32),
            jax.ShapeDtypeStruct((peers, per, width), f32),
        ),
        in_specs=[pl.BlockSpec(memory_space=pltpu.SMEM)] + [vmem] * 3 + [pl.BlockSpec(memory_space=pl.ANY)],
        out_specs=(vmem,) * 3,
        scratch_shapes=[
            pltpu.VMEM((peers, per, width), f32),
            pltpu.VMEM((8, rows), f32),
            pltpu.VMEM((2, peers, per, width), f32),
            pltpu.VMEM((2, halves, width, piece), bf16),
            pltpu.VMEM((2, halves, width, piece), bf16),
            pltpu.VMEM((2, near, rows, width), f32),
            pltpu.VMEM((2, near, rows, width), bf16),
            pltpu.VMEM((2, near, rows, width), bf16),
            pltpu.VMEM((2, near, 8, rows), f32),
            pltpu.VMEM((max(2 * count * blocks * rows // width, table.shape[0]), width), f32),
            pltpu.VMEM((2, halves, 2, near, 8, rows), f32),
            pltpu.VMEM((blocks, 2 * blocks, rows), f32),
            pltpu.VMEM((blocks, max(8, blocks), rows), f32),
            pltpu.VMEM((2, 8, rows), f32),
            pltpu.VMEM((2, near, 8, rows), f32),
            pltpu.VMEM((2, peers, per, width), f32),
            pltpu.VMEM((2, peers, per, width), f32),
            pltpu.VMEM((2, near, width, rows), f32),
            pltpu.VMEM((near, width, rows), f32),
            pltpu.VMEM((near, width, rows), f32),
            pltpu.SemaphoreType.DMA, pairs, pairs, nears, nears, nears, nears, nears, nears, nears, nears,
            crews, crews, crews, crews, pltpu.SemaphoreType.DMA, pltpu.SemaphoreType.DMA,
            pairs, pairs, nears, nears, nears, nears,
        ],
        compiler_params=pltpu.CompilerParams(
            collective_id=0, has_side_effects=True, vmem_limit_bytes=67043328
        ),
        cost_estimate=pl.CostEstimate(flops=flops, bytes_accessed=4 * count * width, transcendentals=0),
    )(ids, pos_ids.reshape(1, rows), dloss.reshape(1, rows), hidden, table)
    items = table.shape[0]
    chunk = math.gcd(512, items)
    whole = lambda *shape: pl.BlockSpec(shape, lambda i: (0,) * len(shape))
    loss, grad_hidden, grad_table = pl.pallas_call(
        scatter,
        grid=(items // chunk,),
        out_shape=(
            jax.ShapeDtypeStruct((1, rows), f32),
            jax.ShapeDtypeStruct((rows, width), f32),
            jax.ShapeDtypeStruct(table.shape, f32),
        ),
        in_specs=[whole(1, count), whole(1, rows), whole(rows, width), whole(count, width)],
        out_specs=(whole(1, rows), whole(rows, width), pl.BlockSpec((chunk, width), lambda i: (i, 0))),
        scratch_shapes=[pltpu.VMEM((2 * count, width), bf16)],
        cost_estimate=pl.CostEstimate(
            flops=4 * items * count * width, bytes_accessed=4 * items * width, transcendentals=0
        ),
    )(ids.reshape(1, count), loss, grad_hidden, returned.reshape(count, width))
    return (loss.reshape(rows), grad_hidden, grad_table)


def solution(mesh):
    in_specs = (
        P(("dp", "table"), None),
        P(("dp", "table"), None),
        P("dp", "table", None, None),
        P(("dp", "table")),
        P(("dp", "table")),
    )
    out_specs = (P(("dp", "table")), P(("dp", "table"), None), P(("dp", "table"), None))
    return jax.shard_map(local, mesh=mesh, in_specs=in_specs, out_specs=out_specs, check_vma=False)
```

```python
import functools
import math

import jax
import jax.numpy as jnp
from jax import lax
from jax.experimental import pallas as pl
from jax.experimental.pallas import tpu as pltpu
from jax.sharding import PartitionSpec as P

MESH = pl.DeviceIdType.MESH


def split(x):
    high = x.astype(jnp.bfloat16)
    return high, (x - high.astype(jnp.float32)).astype(jnp.bfloat16)


def kernel(
    peers, near, scale,
    ids_ref, pos_ref, dloss_ref, hid_ref, table_ref,
    loss_ref, gh_ref, back_ref,
    out, note, cand, ct_hi, ct_lo, hid, h_hi, h_lo, side, expo, bstat, stat, aim, lossbuf, merged, cg, ret, ght, ghmate, ghrecv,
    table_sem, c_send, c_recv, h_send, h_recv, m_send, m_recv, d_send, d_recv, e_send, e_recv,
    t_send, t_recv, a_send, a_recv, l_send, l_recv, z_send, z_recv, x_send, x_recv, g_send, g_recv,
):
    me = lax.axis_index("dp")
    t = lax.axis_index("table")
    a, k = me // 2, lax.rem(me, 2)
    hi, lo, s = t // (near * 2), lax.rem(t // 2, near), lax.rem(t, 2)
    rows, width = hid_ref.shape
    per = ids_ref.shape[1]
    halves = peers // 2
    count = peers * per
    piece = 2 * per
    blocks = 2 * near
    slices = h_send.shape[1]
    mine = a * 2 + s
    same = s == k
    other = 1 - k
    ln2 = math.log(2.0)
    bend = scale / ln2

    def place(far, mid, last):
        return far * (near * 2) + mid * 2 + last

    def wrap(base, step, size):
        return lax.rem(base + step, size)

    def device(da, dk, dh, dl, ds):
        return (
            wrap(a, da, halves) * 2 + wrap(k, dk, 2),
            place(wrap(hi, dh, 2), wrap(lo, dl, near), wrap(s, ds, 2)),
        )

    items = table_ref.shape[0]
    bring = pltpu.make_async_copy(table_ref, expo.at[pl.ds(0, items)], table_sem)
    bring.start()
    both = (0, 1)
    greet = [
        (da, dk, dh, dl, ds)
        for da in range(halves) for dk in both for dh in both for dl in range(near) for ds in both
        if (da, dk, dh, dl, ds) != (0, 0, 0, 0, 0) and (dl == 0 or (da == 0 and dh == 0))
    ]
    barrier = pltpu.get_barrier_semaphore()
    for g in greet:
        pl.semaphore_signal(barrier, inc=1, device_id=device(*g), device_id_type=MESH)
    note[0:1, :] = pos_ref[...].astype(jnp.float32)
    note[1:2, :] = dloss_ref[...]
    bring.wait()

    def pick(da, dc):
        g = wrap(a, da, halves) * 2 + wrap(s, dc, 2)

        def row(i, carry):
            out[g, pl.ds(i, 1), :] = expo[pl.ds(ids_ref[g, i], 1), :]
            return carry

        lax.fori_loop(0, per, row, 0, unroll=8)

    for da in range(halves - 1, -1, -1):
        for dc in both:
            pick(da, dc)
    pl.semaphore_wait(barrier, len(greet))

    started = []

    def send(src, dst, ssem, rsem, dev, own=None):
        copy = pltpu.make_async_remote_copy(
            src_ref=src, dst_ref=dst, send_sem=ssem, recv_sem=rsem, device_id=dev, device_id_type=MESH
        )
        if own is None:
            copy.start()
        else:
            @pl.when(own)
            def _():
                pltpu.make_async_copy(src, dst, rsem).start()

            @pl.when(jnp.logical_not(own))
            def _():
                copy.start()
        started.append((copy, own))

    def arrive(dst, rsem):
        pltpu.make_async_copy(dst, dst, rsem).wait()

    def send_cand(dh, da, dc):
        to = wrap(a, da, halves)
        g = to * 2 + wrap(s, dc, 2)
        send(
            out.at[g], cand.at[dh, me], c_send.at[dh, g], c_recv.at[dh, me],
            (to * 2 + s, place(wrap(hi, dh, 2), lo, wrap(s, dc, 2))),
            same if (dh, da, dc) == (0, 0, 0) else None,
        )

    parts_h = [pl.ds(q * (rows // slices), rows // slices) for q in range(slices)]

    def send_hid(dl):
        dev = (mine, place(hi, lo, k))
        send(note, side.at[s, lo], d_send.at[dl], d_recv.at[lo], dev, same)
        for q, part in enumerate(parts_h):
            send(hid_ref.at[part], hid.at[s, lo, part], h_send.at[dl, q], h_recv.at[lo, q], dev, same)

    later = range(1, near)
    far = range(halves - 1, -1, -1)
    send_hid(0)
    for da in far:
        send_cand(1, da, 0)
    for da in range(halves):
        send_cand(0, da, 0)
    send_cand(1, far[0], 1)

    mate = (a * 2 + other, t)

    def take_hid(dl):
        mid = wrap(lo, dl, near)
        arrive(side.at[k, mid], d_recv.at[mid])
        send(side.at[k, mid], side.at[k, mid], e_send.at[mid], e_recv.at[mid], mate)
        if dl == 0:
            for d in later:
                send(side.at[k, mid], side.at[k, mid], d_send.at[d], d_recv.at[mid], device(0, 0, 0, d, 0))
        for q, part in enumerate(parts_h):
            arrive(hid.at[k, mid, part], h_recv.at[mid, q])
            held = hid.at[k, mid, part]
            if dl == 0:
                for d in later:
                    send(held, held, h_send.at[d, q], h_recv.at[mid, q], device(0, 0, 0, d, 0))
            send(held, held, m_send.at[mid, q], m_recv.at[mid, q], mate)
        cut(k, mid)

    def take_mate(dl):
        mid = wrap(lo, dl, near)
        arrive(side.at[other, mid], e_recv.at[mid])
        for q, part in enumerate(parts_h):
            arrive(hid.at[other, mid, part], m_recv.at[mid, q])
        cut(other, mid)

    def cut(x, mid):
        top, low = split(hid[x, mid] * bend)
        h_hi[x, mid] = top
        h_lo[x, mid] = low

    def hits(dh, j, x, mid):
        base = place(wrap(hi, dh, 2), lo, k) * count + wrap(a, j, halves) * piece
        index = lax.broadcasted_iota(jnp.int32, (piece, rows), 0) + base
        return index == side[x, mid, 0:1, :].astype(jnp.int32)

    def take_cand(dh, j):
        for dk in both:
            source = wrap(a, j, halves) * 2 + wrap(k, dk, 2)
            arrive(cand.at[dh, source], c_recv.at[dh, source])

    folds = rows // width

    def slot(dh, j, x, mid, fold):
        first = ((((dh * halves + j) * 2 + x) * near + mid) * folds + fold) * piece
        return pl.ds(pl.multiple_of(first, piece), piece)

    def keep(dh, j, x, mid, value):
        for fold in range(folds):
            expo[slot(dh, j, x, mid, fold), :] = value[:, fold * width : (fold + 1) * width]

    def kept(dh, j, x, mid):
        return jnp.concatenate([expo[slot(dh, j, x, mid, fold), :] for fold in range(folds)], axis=1)

    def turn(dh, j):
        turned = split(cand[dh, pl.ds(wrap(a, j, halves) * 2, 2)].reshape(piece, width).T)
        ct_hi[dh, j] = turned[0]
        ct_lo[dh, j] = turned[1]

    def forward(dh, j, first, last):
        block = cand[dh, pl.ds(wrap(a, j, halves) * 2, 2)].reshape(piece, width)
        b_hi, b_lo = split(block)
        left = jnp.concatenate([b_hi, b_lo, b_hi], axis=1)

        def step(i, carry):
            x, mid = lax.rem(i, 2), wrap(lo, i // 2, near)
            right = jnp.concatenate([h_hi[x, mid], h_hi[x, mid], h_lo[x, mid]], axis=1)
            logits = lax.dot_general(
                left, right, (((1,), (1,)), ((), ())), preferred_element_type=jnp.float32
            )
            peak = jnp.max(logits, axis=0, keepdims=True)
            power = jnp.exp2(logits - peak)
            keep(dh, j, x, mid, power)
            bstat[dh, j, x, mid, 0:1, :] = peak
            bstat[dh, j, x, mid, 1:2, :] = jnp.sum(power, axis=0, keepdims=True)
            bstat[dh, j, x, mid, 2:3, :] = jnp.sum(
                jnp.where(hits(dh, j, x, mid), logits, 0.0), axis=0, keepdims=True
            )
            return carry

        lax.fori_loop(first, last, step, 0, unroll=2)

    STEPS = [(take_hid, 0), (take_mate, 0)]
    STEPS += [(send_cand, 0, da, 1) for da in range(halves)] + [(send_cand, 1, da, 1) for da in far[1:]]
    for j in range(halves):
        STEPS += [(take_cand, 0, j), (forward, 0, j, 0, 2), (turn, 0, j)]
    STEPS += [(take_cand, 1, far[0]), (forward, 1, far[0], 0, 2), (turn, 1, far[0])]
    STEPS += [(take_hid, dl) for dl in later] + [(take_mate, dl) for dl in later]
    STEPS += [(forward, 0, j, 2, blocks) for j in range(halves)]
    STEPS += [(forward, 1, far[0], 2, blocks)]
    for j in far[1:]:
        STEPS += [(take_cand, 1, j), (forward, 1, j, 0, blocks), (turn, 1, j)]
    for todo in STEPS:
        todo[0](*todo[1:])

    parts = [(dh, j) for dh in both for j in range(halves)]
    seat = k * near + lo
    for x in both:
        for mid in range(near):
            m = x * near + mid
            peak = bstat[0, 0, x, mid, 0:1, :]
            for p in parts[1:]:
                peak = jnp.maximum(peak, bstat[p[0], p[1], x, mid, 0:1, :])
            total = jnp.zeros_like(peak)
            target = jnp.zeros_like(peak)
            for p in parts:
                total += bstat[p[0], p[1], x, mid, 1:2, :] * jnp.exp2(bstat[p[0], p[1], x, mid, 0:1, :] - peak)
                target += bstat[p[0], p[1], x, mid, 2:3, :]
            stat[seat, m : m + 1, :] = peak
            stat[seat, blocks + m : blocks + m + 1, :] = total
            aim[seat, m : m + 1, :] = target
    crew = [(dk, dl) for dl in range(near - 1, -1, -1) for dk in both if (dk, dl) != (0, 0)]
    for dk, dl in crew:
        send(
            stat.at[seat], stat.at[seat], t_send.at[dk, dl], t_recv.at[dk, dl], device(0, dk, 0, dl, 0)
        )
    for dk, dl in crew:
        send(
            aim.at[seat], aim.at[seat], a_send.at[dk, dl], a_recv.at[dk, dl], device(0, dk, 0, dl, 0)
        )
    for dk, dl in crew:
        came = wrap(k, dk, 2) * near + wrap(lo, near - dl, near)
        arrive(stat.at[came], t_recv.at[dk, dl])

    for x in both:
        for mid in range(near):
            m = x * near + mid
            peak = stat[0, m : m + 1, :]
            for w in range(1, blocks):
                peak = jnp.maximum(peak, stat[w, m : m + 1, :])
            total = jnp.zeros_like(peak)
            for w in range(blocks):
                total += stat[w, blocks + m : blocks + m + 1, :] * jnp.exp2(stat[w, m : m + 1, :] - peak)
            weight = ln2 * side[x, mid, 1:2, :]
            merged[x, mid, 0:1, :] = peak
            merged[x, mid, 1:2, :] = weight / total
            merged[x, mid, 2:3, :] = weight
            merged[x, mid, 3:4, :] = ln2 * peak + jnp.log(total)

    def backward(dh, j, first, last, fresh):
        flip = jnp.concatenate([ct_hi[dh, j], ct_hi[dh, j], ct_lo[dh, j]], axis=1)

        def step(i, acc):
            x, mid = lax.rem(i, 2), wrap(lo, i // 2, near)
            weight = merged[x, mid, 2:3, :]
            factor = merged[x, mid, 1:2, :] * jnp.exp2(bstat[dh, j, x, mid, 0:1, :] - merged[x, mid, 0:1, :])
            power = kept(dh, j, x, mid) * factor
            c_hi, c_lo = split(jnp.where(hits(dh, j, x, mid), power - weight, power))
            term = jnp.dot(
                flip, jnp.concatenate([c_hi, c_lo, c_hi], axis=0), preferred_element_type=jnp.float32
            )
            if fresh:
                ght[x, mid] = term
            else:
                ght[x, mid] += term
            return acc + jnp.dot(
                jnp.concatenate([c_hi, c_lo, c_hi], axis=1),
                jnp.concatenate([h_hi[x, mid], h_hi[x, mid], h_lo[x, mid]], axis=0),
                preferred_element_type=jnp.float32,
            )

        start = wrap(a, j, halves) * 2
        if last == blocks:
            acc = jnp.zeros((piece, width), jnp.float32)
        else:
            acc = cg[dh, pl.ds(start, 2)].reshape(piece, width)
        acc = lax.fori_loop(first, last, step, acc, unroll=4 if last - first == 4 else 2)
        cg[dh, pl.ds(start, 2)] = acc.reshape(2, per, width)

    def send_back(dh, j):
        start = wrap(a, j, halves) * 2
        for dk in both:
            source = start + wrap(k, dk, 2)
            send(
                cg.at[dh, source], ret.at[dh, mine], z_send.at[dh, source], z_recv.at[dh, mine],
                (source, place(wrap(hi, dh, 2), lo, k)),
                same if (dh, j, dk) == (0, 0, 0) else None,
            )

    def pass_hid(dl):
        mid = wrap(lo, dl, near)
        send(ght.at[other, mid], ghmate.at[mid], x_send.at[mid], x_recv.at[mid], mate)

    def sum_hid(dl):
        mid = wrap(lo, dl, near)
        arrive(ghmate.at[mid], x_recv.at[mid])
        ght[k, mid] += ghmate[mid]
        send(
            ght.at[k, mid], ghrecv.at[lo], g_send.at[dl], g_recv.at[lo],
            (mine, place(hi, mid, k)), same if dl == 0 else None,
        )

    order = [(1, j) for j in far] + [(0, j) for j in far]
    head, tail = order[0], order[1:]
    STEPS = [(backward, *head, 0, blocks, True), (send_back, *head)]
    STEPS += [(backward, *p, 2, blocks, False) for p in tail]
    STEPS += [(pass_hid, dl) for dl in later]
    STEPS += [(backward, *tail[0], 0, 2, False), (send_back, *tail[0])]
    STEPS += [(sum_hid, dl) for dl in later]
    for p in tail[1:]:
        STEPS += [(backward, *p, 0, 2, False), (send_back, *p)]
    STEPS += [(pass_hid, 0), (sum_hid, 0)]
    for todo in STEPS:
        todo[0](*todo[1:])

    for dk, dl in crew:
        came = wrap(k, dk, 2) * near + wrap(lo, near - dl, near)
        arrive(aim.at[came], a_recv.at[dk, dl])
    target = jnp.zeros((1, rows), jnp.float32)
    for w in range(blocks):
        target += aim[w, pl.ds(seat, 1), :]
    lossbuf[0] = jnp.broadcast_to(merged[k, lo, 3:4, :] - ln2 * target, lossbuf.shape[1:])
    send(lossbuf.at[0], lossbuf.at[1], l_send, l_recv, (mine, place(hi, lo, k)), same)

    for dl in range(near):
        mid = wrap(lo, dl, near)
        arrive(ghrecv.at[mid], g_recv.at[mid])
    whole = ghrecv[0]
    for mid in range(1, near):
        whole += ghrecv[mid]
    gh_ref[...] = (bend * whole).T
    arrive(lossbuf.at[1], l_recv)
    loss_ref[...] = lossbuf[1, 0:1, :]
    for dh in both:
        for g in range(peers):
            arrive(ret.at[dh, g], z_recv.at[dh, g])
    back_ref[...] = ret[0] + ret[1]
    for copy, own in started:
        if own is None:
            copy.wait_send()
        else:
            @pl.when(jnp.logical_not(own))
            def _():
                copy.wait_send()


def scatter(ids_in, loss_in, gh_in, back_in, loss_ref, gh_ref, out_ref, rows, parts, ids, loss, gh, in_sem, out_sem):
    count, chunks = ids.shape[1], out_sem.shape[0] - 2
    chunk = out_ref.shape[0] // chunks
    pairs = ((ids_in, ids), (back_in, parts), (gh_in, gh), (loss_in, loss))
    reads = [pltpu.make_async_copy(src, dst, in_sem.at[n]) for n, (src, dst) in enumerate(pairs)]
    for read in reads:
        read.start()
    writes = []

    def write(src, dst):
        copy = pltpu.make_async_copy(src, dst, out_sem.at[len(writes)])
        copy.start()
        writes.append(copy)

    reads[0].wait()
    reads[1].wait()
    both = jnp.concatenate(split(parts[...]), axis=0)
    for n in range(chunks):
        index = lax.broadcasted_iota(jnp.int32, (chunk, count), 0) + n * chunk
        chosen = (index == ids[...]).astype(jnp.bfloat16)
        part = pl.ds(n * chunk, chunk)
        rows[part] = jnp.dot(jnp.concatenate([chosen, chosen], axis=1), both, preferred_element_type=jnp.float32)
        write(rows.at[part], out_ref.at[part])
        if n == 0:
            reads[2].wait()
            write(gh, gh_ref)
            reads[3].wait()
            write(loss, loss_ref)
    for copy in writes:
        copy.wait()


def local(table, hidden, neg_ids, pos_ids, dloss):
    rows, width = hidden.shape
    scale = 3.0 / math.sqrt(width)
    peers = lax.axis_size("dp")
    near = lax.axis_size("table") // 4
    ids = neg_ids[0, 0]
    per = neg_ids.shape[3]
    count = peers * per
    halves, blocks, piece = peers // 2, 2 * near, 2 * per
    f32, bf16 = jnp.float32, jnp.bfloat16
    pairs = pltpu.SemaphoreType.DMA((2, peers))
    nears = pltpu.SemaphoreType.DMA((near,))
    slices = pltpu.SemaphoreType.DMA((near, 4))
    crews = pltpu.SemaphoreType.DMA((2, near))
    vmem = pl.BlockSpec(memory_space=pltpu.VMEM)
    flops = 18 * 4 * count * near * rows * width
    loss, grad_hidden, returned = pl.pallas_call(
        functools.partial(kernel, peers, near, scale),
        out_shape=(
            jax.ShapeDtypeStruct((1, rows), f32),
            jax.ShapeDtypeStruct((rows, width), f32),
            jax.ShapeDtypeStruct((peers, per, width), f32),
        ),
        in_specs=[pl.BlockSpec(memory_space=pltpu.SMEM)] + [vmem] * 3 + [pl.BlockSpec(memory_space=pl.ANY)],
        out_specs=(vmem,) * 3,
        scratch_shapes=[
            pltpu.VMEM((peers, per, width), f32),
            pltpu.VMEM((8, rows), f32),
            pltpu.VMEM((2, peers, per, width), f32),
            pltpu.VMEM((2, halves, width, piece), bf16),
            pltpu.VMEM((2, halves, width, piece), bf16),
            pltpu.VMEM((2, near, rows, width), f32),
            pltpu.VMEM((2, near, rows, width), bf16),
            pltpu.VMEM((2, near, rows, width), bf16),
            pltpu.VMEM((2, near, 8, rows), f32),
            pltpu.VMEM((max(2 * count * blocks * rows // width, table.shape[0]), width), f32),
            pltpu.VMEM((2, halves, 2, near, 8, rows), f32),
            pltpu.VMEM((blocks, 2 * blocks, rows), f32),
            pltpu.VMEM((blocks, max(8, blocks), rows), f32),
            pltpu.VMEM((2, 8, rows), f32),
            pltpu.VMEM((2, near, 8, rows), f32),
            pltpu.VMEM((2, peers, per, width), f32),
            pltpu.VMEM((2, peers, per, width), f32),
            pltpu.VMEM((2, near, width, rows), f32),
            pltpu.VMEM((near, width, rows), f32),
            pltpu.VMEM((near, width, rows), f32),
            pltpu.SemaphoreType.DMA, pairs, pairs, slices, slices, slices, slices, nears, nears, nears, nears,
            crews, crews, crews, crews, pltpu.SemaphoreType.DMA, pltpu.SemaphoreType.DMA,
            pairs, pairs, nears, nears, nears, nears,
        ],
        compiler_params=pltpu.CompilerParams(
            collective_id=0, has_side_effects=True, vmem_limit_bytes=67043328
        ),
        cost_estimate=pl.CostEstimate(flops=flops, bytes_accessed=4 * count * width, transcendentals=0),
    )(ids, pos_ids.reshape(1, rows), dloss.reshape(1, rows), hidden, table)
    items = table.shape[0]
    chunks = items // math.gcd(512, items)
    anywhere = pl.BlockSpec(memory_space=pl.ANY)
    loss, grad_hidden, grad_table = pl.pallas_call(
        scatter,
        out_shape=(
            jax.ShapeDtypeStruct((1, rows), f32),
            jax.ShapeDtypeStruct((rows, width), f32),
            jax.ShapeDtypeStruct(table.shape, f32),
        ),
        in_specs=[anywhere] * 4,
        out_specs=(anywhere,) * 3,
        scratch_shapes=[
            pltpu.VMEM(table.shape, f32),
            pltpu.VMEM((count, width), f32),
            pltpu.VMEM((1, count), jnp.int32),
            pltpu.VMEM((1, rows), f32),
            pltpu.VMEM((rows, width), f32),
            pltpu.SemaphoreType.DMA((4,)),
            pltpu.SemaphoreType.DMA((chunks + 2,)),
        ],
        compiler_params=pltpu.CompilerParams(vmem_limit_bytes=67043328),
        cost_estimate=pl.CostEstimate(
            flops=4 * items * count * width, bytes_accessed=4 * items * width, transcendentals=0
        ),
    )(ids.reshape(1, count), loss, grad_hidden, returned.reshape(count, width))
    return (loss.reshape(rows), grad_hidden, grad_table)


def solution(mesh):
    in_specs = (
        P(("dp", "table"), None),
        P(("dp", "table"), None),
        P("dp", "table", None, None),
        P(("dp", "table")),
        P(("dp", "table")),
    )
    out_specs = (P(("dp", "table")), P(("dp", "table"), None), P(("dp", "table"), None))
    return jax.shard_map(local, mesh=mesh, in_specs=in_specs, out_specs=out_specs, check_vma=False)
```

```python
import functools
import math

import jax
import jax.numpy as jnp
from jax import lax
from jax.experimental import pallas as pl
from jax.experimental.pallas import tpu as pltpu
from jax.sharding import PartitionSpec as P

MESH = pl.DeviceIdType.MESH


def split(x):
    high = x.astype(jnp.bfloat16)
    return high, (x - high.astype(jnp.float32)).astype(jnp.bfloat16)


def kernel(
    peers, near, scale,
    ids_ref, pos_ref, dloss_ref, hid_ref, table_ref,
    loss_ref, gh_ref, back_ref,
    out, note, cand, ct_hi, ct_lo, hid, h_hi, h_lo, side, expo, bstat, stat, aim, lossbuf, merged, cg, ret, ght, ghmate, ghrecv,
    table_sem, c_send, c_recv, h_send, h_recv, m_send, m_recv, d_send, d_recv, e_send, e_recv,
    t_send, t_recv, a_send, a_recv, l_send, l_recv, z_send, z_recv, x_send, x_recv, g_send, g_recv,
):
    me = lax.axis_index("dp")
    t = lax.axis_index("table")
    a, k = me // 2, lax.rem(me, 2)
    hi, lo, s = t // (near * 2), lax.rem(t // 2, near), lax.rem(t, 2)
    rows, width = hid_ref.shape
    per = ids_ref.shape[1]
    halves = peers // 2
    count = peers * per
    piece = 2 * per
    blocks = 2 * near
    slices = h_send.shape[1]
    mine = a * 2 + s
    same = s == k
    other = 1 - k
    ln2 = math.log(2.0)
    bend = scale / ln2

    def place(far, mid, last):
        return far * (near * 2) + mid * 2 + last

    def wrap(base, step, size):
        return lax.rem(base + step, size)

    def device(da, dk, dh, dl, ds):
        return (
            wrap(a, da, halves) * 2 + wrap(k, dk, 2),
            place(wrap(hi, dh, 2), wrap(lo, dl, near), wrap(s, ds, 2)),
        )

    items = table_ref.shape[0]
    bring = pltpu.make_async_copy(table_ref, expo.at[pl.ds(0, items)], table_sem)
    bring.start()
    both = (0, 1)
    greet = [
        (da, dk, dh, dl, ds)
        for da in range(halves) for dk in both for dh in both for dl in range(near) for ds in both
        if (da, dk, dh, dl, ds) != (0, 0, 0, 0, 0) and (dl == 0 or (da == 0 and dh == 0))
    ]
    barrier = pltpu.get_barrier_semaphore()
    for g in greet:
        pl.semaphore_signal(barrier, inc=1, device_id=device(*g), device_id_type=MESH)
    note[0:1, :] = pos_ref[...].astype(jnp.float32)
    note[1:2, :] = dloss_ref[...]
    bring.wait()

    def pick(da, dc):
        g = wrap(a, da, halves) * 2 + wrap(s, dc, 2)

        def row(i, carry):
            out[g, pl.ds(i, 1), :] = expo[pl.ds(ids_ref[g, i], 1), :]
            return carry

        lax.fori_loop(0, per, row, 0, unroll=8)

    for da in range(halves - 1, -1, -1):
        for dc in both:
            pick(da, dc)
    pl.semaphore_wait(barrier, len(greet))

    started = []

    def send(src, dst, ssem, rsem, dev, own=None):
        copy = pltpu.make_async_remote_copy(
            src_ref=src, dst_ref=dst, send_sem=ssem, recv_sem=rsem, device_id=dev, device_id_type=MESH
        )
        if own is None:
            copy.start()
        else:
            @pl.when(own)
            def _():
                pltpu.make_async_copy(src, dst, rsem).start()

            @pl.when(jnp.logical_not(own))
            def _():
                copy.start()
        started.append((copy, own))

    def arrive(dst, rsem):
        pltpu.make_async_copy(dst, dst, rsem).wait()

    def send_cand(dh, da, dc):
        to = wrap(a, da, halves)
        g = to * 2 + wrap(s, dc, 2)
        send(
            out.at[g], cand.at[dh, me], c_send.at[dh, g], c_recv.at[dh, me],
            (to * 2 + s, place(wrap(hi, dh, 2), lo, wrap(s, dc, 2))),
            same if (dh, da, dc) == (0, 0, 0) else None,
        )

    parts_h = [pl.ds(q * (rows // slices), rows // slices) for q in range(slices)]

    def send_hid(dl):
        dev = (mine, place(hi, lo, k))
        send(note, side.at[s, lo], d_send.at[dl], d_recv.at[lo], dev, same)
        for q, part in enumerate(parts_h):
            send(hid_ref.at[part], hid.at[s, lo, part], h_send.at[dl, q], h_recv.at[lo, q], dev, same)

    later = range(1, near)
    far = range(halves - 1, -1, -1)
    send_hid(0)
    for da in far:
        send_cand(1, da, 0)
    for da in range(halves):
        send_cand(0, da, 0)
    send_cand(1, far[0], 1)

    mate = (a * 2 + other, t)

    def take_hid(dl):
        mid = wrap(lo, dl, near)
        arrive(side.at[k, mid], d_recv.at[mid])
        send(side.at[k, mid], side.at[k, mid], e_send.at[mid], e_recv.at[mid], mate)
        if dl == 0:
            for d in later:
                send(side.at[k, mid], side.at[k, mid], d_send.at[d], d_recv.at[mid], device(0, 0, 0, d, 0))
        for q, part in enumerate(parts_h):
            arrive(hid.at[k, mid, part], h_recv.at[mid, q])
            held = hid.at[k, mid, part]
            if dl == 0:
                for d in later:
                    send(held, held, h_send.at[d, q], h_recv.at[mid, q], device(0, 0, 0, d, 0))
            send(held, held, m_send.at[mid, q], m_recv.at[mid, q], mate)
        cut(k, mid)

    def take_mate(dl):
        mid = wrap(lo, dl, near)
        arrive(side.at[other, mid], e_recv.at[mid])
        for q, part in enumerate(parts_h):
            arrive(hid.at[other, mid, part], m_recv.at[mid, q])
        cut(other, mid)

    def cut(x, mid):
        top, low = split(hid[x, mid] * bend)
        h_hi[x, mid] = top
        h_lo[x, mid] = low

    def hits(dh, j, x, mid):
        base = place(wrap(hi, dh, 2), lo, k) * count + wrap(a, j, halves) * piece
        index = lax.broadcasted_iota(jnp.int32, (piece, rows), 0) + base
        return index == side[x, mid, 0:1, :].astype(jnp.int32)

    def take_cand(dh, j):
        for dk in both:
            source = wrap(a, j, halves) * 2 + wrap(k, dk, 2)
            arrive(cand.at[dh, source], c_recv.at[dh, source])

    folds = rows // width

    def slot(dh, j, x, mid, fold):
        first = ((((dh * halves + j) * 2 + x) * near + mid) * folds + fold) * piece
        return pl.ds(pl.multiple_of(first, piece), piece)

    def keep(dh, j, x, mid, value):
        for fold in range(folds):
            expo[slot(dh, j, x, mid, fold), :] = value[:, fold * width : (fold + 1) * width]

    def kept(dh, j, x, mid):
        return jnp.concatenate([expo[slot(dh, j, x, mid, fold), :] for fold in range(folds)], axis=1)

    def turn(dh, j):
        turned = split(cand[dh, pl.ds(wrap(a, j, halves) * 2, 2)].reshape(piece, width).T)
        ct_hi[dh, j] = turned[0]
        ct_lo[dh, j] = turned[1]

    def forward(dh, j, first, last):
        block = cand[dh, pl.ds(wrap(a, j, halves) * 2, 2)].reshape(piece, width)
        b_hi, b_lo = split(block)
        left = jnp.concatenate([b_hi, b_lo, b_hi], axis=1)

        def step(i, carry):
            x, mid = lax.rem(i, 2), wrap(lo, i // 2, near)
            right = jnp.concatenate([h_hi[x, mid], h_hi[x, mid], h_lo[x, mid]], axis=1)
            logits = lax.dot_general(
                left, right, (((1,), (1,)), ((), ())), preferred_element_type=jnp.float32
            )
            peak = jnp.max(logits, axis=0, keepdims=True)
            power = jnp.exp2(logits - peak)
            keep(dh, j, x, mid, power)
            bstat[dh, j, x, mid, 0:1, :] = peak
            bstat[dh, j, x, mid, 1:2, :] = jnp.sum(power, axis=0, keepdims=True)
            bstat[dh, j, x, mid, 2:3, :] = jnp.sum(
                jnp.where(hits(dh, j, x, mid), logits, 0.0), axis=0, keepdims=True
            )
            return carry

        lax.fori_loop(first, last, step, 0, unroll=2)

    STEPS = [(take_hid, 0), (take_mate, 0)]
    STEPS += [(send_cand, 0, da, 1) for da in range(halves)] + [(send_cand, 1, da, 1) for da in far[1:]]
    for j in range(halves):
        STEPS += [(take_cand, 0, j), (forward, 0, j, 0, 2), (turn, 0, j)]
    STEPS += [(take_cand, 1, far[0]), (forward, 1, far[0], 0, 2), (turn, 1, far[0])]
    STEPS += [(take_hid, dl) for dl in later] + [(take_mate, dl) for dl in later]
    STEPS += [(forward, 0, j, 2, blocks) for j in range(halves)]
    STEPS += [(forward, 1, far[0], 2, blocks)]
    for j in far[1:]:
        STEPS += [(take_cand, 1, j), (forward, 1, j, 0, blocks), (turn, 1, j)]
    for todo in STEPS:
        todo[0](*todo[1:])

    parts = [(dh, j) for dh in both for j in range(halves)]
    seat = k * near + lo
    for x in both:
        for mid in range(near):
            m = x * near + mid
            peak = bstat[0, 0, x, mid, 0:1, :]
            for p in parts[1:]:
                peak = jnp.maximum(peak, bstat[p[0], p[1], x, mid, 0:1, :])
            total = jnp.zeros_like(peak)
            target = jnp.zeros_like(peak)
            for p in parts:
                total += bstat[p[0], p[1], x, mid, 1:2, :] * jnp.exp2(bstat[p[0], p[1], x, mid, 0:1, :] - peak)
                target += bstat[p[0], p[1], x, mid, 2:3, :]
            stat[seat, m : m + 1, :] = peak
            stat[seat, blocks + m : blocks + m + 1, :] = total
            aim[seat, m : m + 1, :] = target
    crew = [(dk, dl) for dl in range(near - 1, -1, -1) for dk in both if (dk, dl) != (0, 0)]
    for dk, dl in crew:
        send(
            stat.at[seat], stat.at[seat], t_send.at[dk, dl], t_recv.at[dk, dl], device(0, dk, 0, dl, 0)
        )
    for dk, dl in crew:
        send(
            aim.at[seat], aim.at[seat], a_send.at[dk, dl], a_recv.at[dk, dl], device(0, dk, 0, dl, 0)
        )
    for dk, dl in crew:
        came = wrap(k, dk, 2) * near + wrap(lo, near - dl, near)
        arrive(stat.at[came], t_recv.at[dk, dl])

    for x in both:
        for mid in range(near):
            m = x * near + mid
            peak = stat[0, m : m + 1, :]
            for w in range(1, blocks):
                peak = jnp.maximum(peak, stat[w, m : m + 1, :])
            total = jnp.zeros_like(peak)
            for w in range(blocks):
                total += stat[w, blocks + m : blocks + m + 1, :] * jnp.exp2(stat[w, m : m + 1, :] - peak)
            weight = ln2 * side[x, mid, 1:2, :]
            merged[x, mid, 0:1, :] = peak
            merged[x, mid, 1:2, :] = weight / total
            merged[x, mid, 2:3, :] = weight
            merged[x, mid, 3:4, :] = ln2 * peak + jnp.log(total)

    def backward(dh, j, first, last, fresh):
        flip = jnp.concatenate([ct_hi[dh, j], ct_hi[dh, j], ct_lo[dh, j]], axis=1)

        def step(i, acc):
            x, mid = lax.rem(i, 2), wrap(lo, i // 2, near)
            weight = merged[x, mid, 2:3, :]
            factor = merged[x, mid, 1:2, :] * jnp.exp2(bstat[dh, j, x, mid, 0:1, :] - merged[x, mid, 0:1, :])
            power = kept(dh, j, x, mid) * factor
            c_hi, c_lo = split(jnp.where(hits(dh, j, x, mid), power - weight, power))
            term = jnp.dot(
                flip, jnp.concatenate([c_hi, c_lo, c_hi], axis=0), preferred_element_type=jnp.float32
            )
            if fresh:
                ght[x, mid] = term
            else:
                ght[x, mid] += term
            return acc + jnp.dot(
                jnp.concatenate([c_hi, c_lo, c_hi], axis=1),
                jnp.concatenate([h_hi[x, mid], h_hi[x, mid], h_lo[x, mid]], axis=0),
                preferred_element_type=jnp.float32,
            )

        start = wrap(a, j, halves) * 2
        if last == blocks:
            acc = jnp.zeros((piece, width), jnp.float32)
        else:
            acc = cg[dh, pl.ds(start, 2)].reshape(piece, width)
        acc = lax.fori_loop(first, last, step, acc, unroll=4 if last - first == 4 else 2)
        cg[dh, pl.ds(start, 2)] = acc.reshape(2, per, width)

    def send_back(dh, j):
        start = wrap(a, j, halves) * 2
        for dk in both:
            source = start + wrap(k, dk, 2)
            send(
                cg.at[dh, source], ret.at[dh, mine], z_send.at[dh, source], z_recv.at[dh, mine],
                (source, place(wrap(hi, dh, 2), lo, k)),
                same if (dh, j, dk) == (0, 0, 0) else None,
            )

    slices = g_send.shape[1]
    parts_g = [pl.ds(q * (width // slices), width // slices) for q in range(slices)]

    def pass_hid(dl):
        mid = wrap(lo, dl, near)
        send(ght.at[other, mid], ghmate.at[mid], x_send.at[mid], x_recv.at[mid], mate)

    def sum_hid(dl):
        mid = wrap(lo, dl, near)
        arrive(ghmate.at[mid], x_recv.at[mid])
        ght[k, mid] += ghmate[mid]
        for q, part in enumerate(parts_g):
            send(
                ght.at[k, mid, part], ghrecv.at[lo, part], g_send.at[dl, q], g_recv.at[lo, q],
                (mine, place(hi, mid, k)), same if dl == 0 else None,
            )

    order = [(1, j) for j in far] + [(0, j) for j in far]
    head, tail = order[0], order[1:]
    STEPS = [(backward, *p, 2, blocks, p == head) for p in order]
    STEPS += [(pass_hid, dl) for dl in later]
    STEPS += [(backward, *head, 0, 2, 2), (send_back, *head)]
    STEPS += [(sum_hid, dl) for dl in later]
    for p in tail:
        STEPS += [(backward, *p, 0, 2, False), (send_back, *p)]
    STEPS += [(pass_hid, 0), (sum_hid, 0)]
    for todo in STEPS:
        todo[0](*todo[1:])

    for dk, dl in crew:
        came = wrap(k, dk, 2) * near + wrap(lo, near - dl, near)
        arrive(aim.at[came], a_recv.at[dk, dl])
    target = jnp.zeros((1, rows), jnp.float32)
    for w in range(blocks):
        target += aim[w, pl.ds(seat, 1), :]
    lossbuf[0] = jnp.broadcast_to(merged[k, lo, 3:4, :] - ln2 * target, lossbuf.shape[1:])
    send(lossbuf.at[0], lossbuf.at[1], l_send, l_recv, (mine, place(hi, lo, k)), same)

    for dl in range(near):
        mid = wrap(lo, dl, near)
        for q, part in enumerate(parts_g):
            arrive(ghrecv.at[mid, part], g_recv.at[mid, q])
    whole = ghrecv[0]
    for mid in range(1, near):
        whole += ghrecv[mid]
    gh_ref[...] = (bend * whole).T
    arrive(lossbuf.at[1], l_recv)
    loss_ref[...] = lossbuf[1, 0:1, :]
    for dh in both:
        for g in range(peers):
            arrive(ret.at[dh, g], z_recv.at[dh, g])
    back_ref[...] = ret[0] + ret[1]
    for copy, own in started:
        if own is None:
            copy.wait_send()
        else:
            @pl.when(jnp.logical_not(own))
            def _():
                copy.wait_send()


def scatter(ids_in, loss_in, gh_in, back_in, loss_ref, gh_ref, out_ref, rows, parts, ids, loss, gh, in_sem, out_sem):
    count, chunks = ids.shape[1], out_sem.shape[0] - 2
    chunk = out_ref.shape[0] // chunks
    pairs = ((ids_in, ids), (back_in, parts), (gh_in, gh), (loss_in, loss))
    reads = [pltpu.make_async_copy(src, dst, in_sem.at[n]) for n, (src, dst) in enumerate(pairs)]
    for read in reads:
        read.start()
    writes = []

    def write(src, dst):
        copy = pltpu.make_async_copy(src, dst, out_sem.at[len(writes)])
        copy.start()
        writes.append(copy)

    reads[0].wait()
    reads[1].wait()
    both = jnp.concatenate(split(parts[...]), axis=0)
    for n in range(chunks):
        index = lax.broadcasted_iota(jnp.int32, (chunk, count), 0) + n * chunk
        chosen = (index == ids[...]).astype(jnp.bfloat16)
        part = pl.ds(n * chunk, chunk)
        rows[part] = jnp.dot(jnp.concatenate([chosen, chosen], axis=1), both, preferred_element_type=jnp.float32)
        write(rows.at[part], out_ref.at[part])
        if n == 0:
            reads[2].wait()
            write(gh, gh_ref)
            reads[3].wait()
            write(loss, loss_ref)
    for copy in writes:
        copy.wait()


def local(table, hidden, neg_ids, pos_ids, dloss):
    rows, width = hidden.shape
    scale = 3.0 / math.sqrt(width)
    peers = lax.axis_size("dp")
    near = lax.axis_size("table") // 4
    ids = neg_ids[0, 0]
    per = neg_ids.shape[3]
    count = peers * per
    halves, blocks, piece = peers // 2, 2 * near, 2 * per
    f32, bf16 = jnp.float32, jnp.bfloat16
    pairs = pltpu.SemaphoreType.DMA((2, peers))
    nears = pltpu.SemaphoreType.DMA((near,))
    slices = pltpu.SemaphoreType.DMA((near, 4))
    crews = pltpu.SemaphoreType.DMA((2, near))
    vmem = pl.BlockSpec(memory_space=pltpu.VMEM)
    flops = 18 * 4 * count * near * rows * width
    loss, grad_hidden, returned = pl.pallas_call(
        functools.partial(kernel, peers, near, scale),
        out_shape=(
            jax.ShapeDtypeStruct((1, rows), f32),
            jax.ShapeDtypeStruct((rows, width), f32),
            jax.ShapeDtypeStruct((peers, per, width), f32),
        ),
        in_specs=[pl.BlockSpec(memory_space=pltpu.SMEM)] + [vmem] * 3 + [pl.BlockSpec(memory_space=pl.ANY)],
        out_specs=(vmem,) * 3,
        scratch_shapes=[
            pltpu.VMEM((peers, per, width), f32),
            pltpu.VMEM((8, rows), f32),
            pltpu.VMEM((2, peers, per, width), f32),
            pltpu.VMEM((2, halves, width, piece), bf16),
            pltpu.VMEM((2, halves, width, piece), bf16),
            pltpu.VMEM((2, near, rows, width), f32),
            pltpu.VMEM((2, near, rows, width), bf16),
            pltpu.VMEM((2, near, rows, width), bf16),
            pltpu.VMEM((2, near, 8, rows), f32),
            pltpu.VMEM((max(2 * count * blocks * rows // width, table.shape[0]), width), f32),
            pltpu.VMEM((2, halves, 2, near, 8, rows), f32),
            pltpu.VMEM((blocks, 2 * blocks, rows), f32),
            pltpu.VMEM((blocks, max(8, blocks), rows), f32),
            pltpu.VMEM((2, 8, rows), f32),
            pltpu.VMEM((2, near, 8, rows), f32),
            pltpu.VMEM((2, peers, per, width), f32),
            pltpu.VMEM((2, peers, per, width), f32),
            pltpu.VMEM((2, near, width, rows), f32),
            pltpu.VMEM((near, width, rows), f32),
            pltpu.VMEM((near, width, rows), f32),
            pltpu.SemaphoreType.DMA, pairs, pairs, slices, slices, slices, slices, nears, nears, nears, nears,
            crews, crews, crews, crews, pltpu.SemaphoreType.DMA, pltpu.SemaphoreType.DMA,
            pairs, pairs, nears, nears, slices, slices,
        ],
        compiler_params=pltpu.CompilerParams(
            collective_id=0, has_side_effects=True, vmem_limit_bytes=67043328
        ),
        cost_estimate=pl.CostEstimate(flops=flops, bytes_accessed=4 * count * width, transcendentals=0),
    )(ids, pos_ids.reshape(1, rows), dloss.reshape(1, rows), hidden, table)
    items = table.shape[0]
    chunks = items // math.gcd(512, items)
    anywhere = pl.BlockSpec(memory_space=pl.ANY)
    loss, grad_hidden, grad_table = pl.pallas_call(
        scatter,
        out_shape=(
            jax.ShapeDtypeStruct((1, rows), f32),
            jax.ShapeDtypeStruct((rows, width), f32),
            jax.ShapeDtypeStruct(table.shape, f32),
        ),
        in_specs=[anywhere] * 4,
        out_specs=(anywhere,) * 3,
        scratch_shapes=[
            pltpu.VMEM(table.shape, f32),
            pltpu.VMEM((count, width), f32),
            pltpu.VMEM((1, count), jnp.int32),
            pltpu.VMEM((1, rows), f32),
            pltpu.VMEM((rows, width), f32),
            pltpu.SemaphoreType.DMA((4,)),
            pltpu.SemaphoreType.DMA((chunks + 2,)),
        ],
        compiler_params=pltpu.CompilerParams(vmem_limit_bytes=67043328),
        cost_estimate=pl.CostEstimate(
            flops=4 * items * count * width, bytes_accessed=4 * items * width, transcendentals=0
        ),
    )(ids.reshape(1, count), loss, grad_hidden, returned.reshape(count, width))
    return (loss.reshape(rows), grad_hidden, grad_table)


def solution(mesh):
    in_specs = (
        P(("dp", "table"), None),
        P(("dp", "table"), None),
        P("dp", "table", None, None),
        P(("dp", "table")),
        P(("dp", "table")),
    )
    out_specs = (P(("dp", "table")), P(("dp", "table"), None), P(("dp", "table"), None))
    return jax.shard_map(local, mesh=mesh, in_specs=in_specs, out_specs=out_specs, check_vma=False)
```

```python
import functools
import math

import jax
import jax.numpy as jnp
from jax import lax
from jax.experimental import pallas as pl
from jax.experimental.pallas import tpu as pltpu
from jax.sharding import PartitionSpec as P

MESH = pl.DeviceIdType.MESH


def split(x):
    high = x.astype(jnp.bfloat16)
    return high, (x - high.astype(jnp.float32)).astype(jnp.bfloat16)


def kernel(
    peers, near, scale,
    ids_ref, pos_ref, dloss_ref, hid_ref, table_ref,
    loss_ref, gh_ref, back_ref,
    out, note, cand, ct_hi, ct_lo, hid, h_hi, h_lo, side, expo, bstat, stat, aim, lossbuf, merged, cg, ret, ght, ghmate, ghrecv,
    table_sem, c_send, c_recv, h_send, h_recv, m_send, m_recv, d_send, d_recv, e_send, e_recv,
    t_send, t_recv, a_send, a_recv, l_send, l_recv, z_send, z_recv, x_send, x_recv, g_send, g_recv,
):
    me = lax.axis_index("dp")
    t = lax.axis_index("table")
    a, k = me // 2, lax.rem(me, 2)
    hi, lo, s = t // (near * 2), lax.rem(t // 2, near), lax.rem(t, 2)
    rows, width = hid_ref.shape
    per = ids_ref.shape[1]
    halves = peers // 2
    count = peers * per
    piece = 2 * per
    blocks = 2 * near
    slices = h_send.shape[1]
    mine = a * 2 + s
    same = s == k
    other = 1 - k
    ln2 = math.log(2.0)
    bend = scale / ln2

    def place(far, mid, last):
        return far * (near * 2) + mid * 2 + last

    def wrap(base, step, size):
        return lax.rem(base + step, size)

    def device(da, dk, dh, dl, ds):
        return (
            wrap(a, da, halves) * 2 + wrap(k, dk, 2),
            place(wrap(hi, dh, 2), wrap(lo, dl, near), wrap(s, ds, 2)),
        )

    items = table_ref.shape[0]
    bring = pltpu.make_async_copy(table_ref, expo.at[pl.ds(0, items)], table_sem)
    bring.start()
    both = (0, 1)
    greet = [
        (da, dk, dh, dl, ds)
        for da in range(halves) for dk in both for dh in both for dl in range(near) for ds in both
        if (da, dk, dh, dl, ds) != (0, 0, 0, 0, 0) and (dl == 0 or (da == 0 and dh == 0))
    ]
    barrier = pltpu.get_barrier_semaphore()
    for g in greet:
        pl.semaphore_signal(barrier, inc=1, device_id=device(*g), device_id_type=MESH)
    note[0:1, :] = pos_ref[...].astype(jnp.float32)
    note[1:2, :] = dloss_ref[...]
    bring.wait()

    def pick(da, dc):
        g = wrap(a, da, halves) * 2 + wrap(s, dc, 2)

        def row(i, carry):
            out[g, pl.ds(i, 1), :] = expo[pl.ds(ids_ref[g, i], 1), :]
            return carry

        lax.fori_loop(0, per, row, 0, unroll=8)

    for da in range(halves - 1, -1, -1):
        for dc in both:
            pick(da, dc)
    pl.semaphore_wait(barrier, len(greet))

    started = []

    def send(src, dst, ssem, rsem, dev, own=None):
        copy = pltpu.make_async_remote_copy(
            src_ref=src, dst_ref=dst, send_sem=ssem, recv_sem=rsem, device_id=dev, device_id_type=MESH
        )
        if own is None:
            copy.start()
        else:
            @pl.when(own)
            def _():
                pltpu.make_async_copy(src, dst, rsem).start()

            @pl.when(jnp.logical_not(own))
            def _():
                copy.start()
        started.append((copy, own))

    def arrive(dst, rsem):
        pltpu.make_async_copy(dst, dst, rsem).wait()

    def send_cand(dh, da, dc):
        to = wrap(a, da, halves)
        g = to * 2 + wrap(s, dc, 2)
        send(
            out.at[g], cand.at[dh, me], c_send.at[dh, g], c_recv.at[dh, me],
            (to * 2 + s, place(wrap(hi, dh, 2), lo, wrap(s, dc, 2))),
            same if (dh, da, dc) == (0, 0, 0) else None,
        )

    parts_h = [pl.ds(q * (rows // slices), rows // slices) for q in range(slices)]

    def send_hid(dl):
        dev = (mine, place(hi, lo, k))
        send(note, side.at[s, lo], d_send.at[dl], d_recv.at[lo], dev, same)
        for q, part in enumerate(parts_h):
            send(hid_ref.at[part], hid.at[s, lo, part], h_send.at[dl, q], h_recv.at[lo, q], dev, same)

    later = range(1, near)
    far = range(halves - 1, -1, -1)
    send_hid(0)
    for da in far:
        send_cand(1, da, 0)
    for da in range(halves):
        send_cand(0, da, 0)
    send_cand(1, far[0], 1)

    mate = (a * 2 + other, t)

    def take_hid(dl):
        mid = wrap(lo, dl, near)
        arrive(side.at[k, mid], d_recv.at[mid])
        send(side.at[k, mid], side.at[k, mid], e_send.at[mid], e_recv.at[mid], mate)
        if dl == 0:
            for d in later:
                send(side.at[k, mid], side.at[k, mid], d_send.at[d], d_recv.at[mid], device(0, 0, 0, d, 0))
        for q, part in enumerate(parts_h):
            arrive(hid.at[k, mid, part], h_recv.at[mid, q])
            held = hid.at[k, mid, part]
            if dl == 0:
                for d in later:
                    send(held, held, h_send.at[d, q], h_recv.at[mid, q], device(0, 0, 0, d, 0))
            send(held, held, m_send.at[mid, q], m_recv.at[mid, q], mate)
        cut(k, mid)

    def take_mate(dl):
        mid = wrap(lo, dl, near)
        arrive(side.at[other, mid], e_recv.at[mid])
        for q, part in enumerate(parts_h):
            arrive(hid.at[other, mid, part], m_recv.at[mid, q])
        cut(other, mid)

    def cut(x, mid):
        top, low = split(hid[x, mid] * bend)
        h_hi[x, mid] = top
        h_lo[x, mid] = low

    def hits(dh, j, x, mid):
        base = place(wrap(hi, dh, 2), lo, k) * count + wrap(a, j, halves) * piece
        index = lax.broadcasted_iota(jnp.int32, (piece, rows), 0) + base
        return index == side[x, mid, 0:1, :].astype(jnp.int32)

    def take_cand(dh, j):
        for dk in both:
            source = wrap(a, j, halves) * 2 + wrap(k, dk, 2)
            arrive(cand.at[dh, source], c_recv.at[dh, source])

    folds = rows // width

    def slot(dh, j, x, mid, fold):
        first = ((((dh * halves + j) * 2 + x) * near + mid) * folds + fold) * piece
        return pl.ds(pl.multiple_of(first, piece), piece)

    def keep(dh, j, x, mid, value):
        for fold in range(folds):
            expo[slot(dh, j, x, mid, fold), :] = value[:, fold * width : (fold + 1) * width]

    def kept(dh, j, x, mid):
        return jnp.concatenate([expo[slot(dh, j, x, mid, fold), :] for fold in range(folds)], axis=1)

    def turn(dh, j):
        turned = split(cand[dh, pl.ds(wrap(a, j, halves) * 2, 2)].reshape(piece, width).T)
        ct_hi[dh, j] = turned[0]
        ct_lo[dh, j] = turned[1]

    def forward(dh, j, first, last):
        block = cand[dh, pl.ds(wrap(a, j, halves) * 2, 2)].reshape(piece, width)
        b_hi, b_lo = split(block)
        left = jnp.concatenate([b_hi, b_lo, b_hi], axis=1)

        def step(i, carry):
            x, mid = lax.rem(i, 2), wrap(lo, i // 2, near)
            right = jnp.concatenate([h_hi[x, mid], h_hi[x, mid], h_lo[x, mid]], axis=1)
            logits = lax.dot_general(
                left, right, (((1,), (1,)), ((), ())), preferred_element_type=jnp.float32
            )
            peak = jnp.max(logits, axis=0, keepdims=True)
            power = jnp.exp2(logits - peak)
            keep(dh, j, x, mid, power)
            bstat[dh, j, x, mid, 0:1, :] = peak
            bstat[dh, j, x, mid, 1:2, :] = jnp.sum(power, axis=0, keepdims=True)
            bstat[dh, j, x, mid, 2:3, :] = jnp.sum(
                jnp.where(hits(dh, j, x, mid), logits, 0.0), axis=0, keepdims=True
            )
            return carry

        lax.fori_loop(first, last, step, 0, unroll=2)

    STEPS = [(take_hid, 0), (take_mate, 0)]
    STEPS += [(send_cand, 0, da, 1) for da in range(halves)] + [(send_cand, 1, da, 1) for da in far[1:]]
    for j in range(halves):
        STEPS += [(take_cand, 0, j), (forward, 0, j, 0, 2), (turn, 0, j)]
    STEPS += [(take_cand, 1, far[0]), (forward, 1, far[0], 0, 2), (turn, 1, far[0])]
    STEPS += [(take_hid, dl) for dl in later] + [(take_mate, dl) for dl in later]
    STEPS += [(forward, 0, j, 2, blocks) for j in range(halves)]
    STEPS += [(forward, 1, far[0], 2, blocks)]
    for j in far[1:]:
        STEPS += [(take_cand, 1, j), (forward, 1, j, 0, blocks)]
    for todo in STEPS:
        todo[0](*todo[1:])

    parts = [(dh, j) for dh in both for j in range(halves)]
    seat = k * near + lo
    for x in both:
        for mid in range(near):
            m = x * near + mid
            peak = bstat[0, 0, x, mid, 0:1, :]
            for p in parts[1:]:
                peak = jnp.maximum(peak, bstat[p[0], p[1], x, mid, 0:1, :])
            total = jnp.zeros_like(peak)
            target = jnp.zeros_like(peak)
            for p in parts:
                total += bstat[p[0], p[1], x, mid, 1:2, :] * jnp.exp2(bstat[p[0], p[1], x, mid, 0:1, :] - peak)
                target += bstat[p[0], p[1], x, mid, 2:3, :]
            stat[seat, m : m + 1, :] = peak
            stat[seat, blocks + m : blocks + m + 1, :] = total
            aim[seat, m : m + 1, :] = target
    crew = [(dk, dl) for dl in range(near - 1, -1, -1) for dk in both if (dk, dl) != (0, 0)]
    for dk, dl in crew:
        send(
            stat.at[seat], stat.at[seat], t_send.at[dk, dl], t_recv.at[dk, dl], device(0, dk, 0, dl, 0)
        )
    for dk, dl in crew:
        send(
            aim.at[seat], aim.at[seat], a_send.at[dk, dl], a_recv.at[dk, dl], device(0, dk, 0, dl, 0)
        )
    for j in far[1:]:
        turn(1, j)
    for dk, dl in crew:
        came = wrap(k, dk, 2) * near + wrap(lo, near - dl, near)
        arrive(stat.at[came], t_recv.at[dk, dl])

    for x in both:
        for mid in range(near):
            m = x * near + mid
            peak = stat[0, m : m + 1, :]
            for w in range(1, blocks):
                peak = jnp.maximum(peak, stat[w, m : m + 1, :])
            total = jnp.zeros_like(peak)
            for w in range(blocks):
                total += stat[w, blocks + m : blocks + m + 1, :] * jnp.exp2(stat[w, m : m + 1, :] - peak)
            weight = ln2 * side[x, mid, 1:2, :]
            merged[x, mid, 0:1, :] = peak
            merged[x, mid, 1:2, :] = weight / total
            merged[x, mid, 2:3, :] = weight
            merged[x, mid, 3:4, :] = ln2 * peak + jnp.log(total)

    def backward(dh, j, first, last, fresh):
        flip = jnp.concatenate([ct_hi[dh, j], ct_hi[dh, j], ct_lo[dh, j]], axis=1)

        def step(i, acc):
            x, mid = lax.rem(i, 2), wrap(lo, i // 2, near)
            weight = merged[x, mid, 2:3, :]
            factor = merged[x, mid, 1:2, :] * jnp.exp2(bstat[dh, j, x, mid, 0:1, :] - merged[x, mid, 0:1, :])
            power = kept(dh, j, x, mid) * factor
            c_hi, c_lo = split(jnp.where(hits(dh, j, x, mid), power - weight, power))
            term = jnp.dot(
                flip, jnp.concatenate([c_hi, c_lo, c_hi], axis=0), preferred_element_type=jnp.float32
            )
            if fresh:
                ght[x, mid] = term
            else:
                ght[x, mid] += term
            return acc + jnp.dot(
                jnp.concatenate([c_hi, c_lo, c_hi], axis=1),
                jnp.concatenate([h_hi[x, mid], h_hi[x, mid], h_lo[x, mid]], axis=0),
                preferred_element_type=jnp.float32,
            )

        start = wrap(a, j, halves) * 2
        if last == blocks:
            acc = jnp.zeros((piece, width), jnp.float32)
        else:
            acc = cg[dh, pl.ds(start, 2)].reshape(piece, width)
        acc = lax.fori_loop(first, last, step, acc, unroll=4 if last - first == 4 else 2)
        cg[dh, pl.ds(start, 2)] = acc.reshape(2, per, width)

    def send_back(dh, j):
        start = wrap(a, j, halves) * 2
        for dk in both:
            source = start + wrap(k, dk, 2)
            send(
                cg.at[dh, source], ret.at[dh, mine], z_send.at[dh, source], z_recv.at[dh, mine],
                (source, place(wrap(hi, dh, 2), lo, k)),
                same if (dh, j, dk) == (0, 0, 0) else None,
            )

    slices = g_send.shape[1]
    parts_g = [pl.ds(q * (width // slices), width // slices) for q in range(slices)]

    def pass_hid(dl):
        mid = wrap(lo, dl, near)
        send(ght.at[other, mid], ghmate.at[mid], x_send.at[mid], x_recv.at[mid], mate)

    def sum_hid(dl):
        mid = wrap(lo, dl, near)
        arrive(ghmate.at[mid], x_recv.at[mid])
        ght[k, mid] += ghmate[mid]
        for q, part in enumerate(parts_g):
            send(
                ght.at[k, mid, part], ghrecv.at[lo, part], g_send.at[dl, q], g_recv.at[lo, q],
                (mine, place(hi, mid, k)), same if dl == 0 else None,
            )

    order = [(1, j) for j in far] + [(0, j) for j in far]
    head, tail = order[0], order[1:]
    STEPS = [(backward, *p, 2, blocks, p == head) for p in order]
    STEPS += [(pass_hid, dl) for dl in later]
    STEPS += [(backward, *head, 0, 2, 2), (send_back, *head)]
    STEPS += [(sum_hid, dl) for dl in later]
    for p in tail:
        STEPS += [(backward, *p, 0, 2, False), (send_back, *p)]
    STEPS += [(pass_hid, 0), (sum_hid, 0)]
    for todo in STEPS:
        todo[0](*todo[1:])

    for dk, dl in crew:
        came = wrap(k, dk, 2) * near + wrap(lo, near - dl, near)
        arrive(aim.at[came], a_recv.at[dk, dl])
    target = jnp.zeros((1, rows), jnp.float32)
    for w in range(blocks):
        target += aim[w, pl.ds(seat, 1), :]
    lossbuf[0] = jnp.broadcast_to(merged[k, lo, 3:4, :] - ln2 * target, lossbuf.shape[1:])
    send(lossbuf.at[0], lossbuf.at[1], l_send, l_recv, (mine, place(hi, lo, k)), same)

    for dl in range(near):
        mid = wrap(lo, dl, near)
        for q, part in enumerate(parts_g):
            arrive(ghrecv.at[mid, part], g_recv.at[mid, q])
    whole = ghrecv[0]
    for mid in range(1, near):
        whole += ghrecv[mid]
    gh_ref[...] = (bend * whole).T
    arrive(lossbuf.at[1], l_recv)
    loss_ref[...] = lossbuf[1, 0:1, :]
    for dh in both:
        for g in range(peers):
            arrive(ret.at[dh, g], z_recv.at[dh, g])
    back_ref[...] = ret[0] + ret[1]
    for copy, own in started:
        if own is None:
            copy.wait_send()
        else:
            @pl.when(jnp.logical_not(own))
            def _():
                copy.wait_send()


def scatter(ids_in, loss_in, gh_in, back_in, loss_ref, gh_ref, out_ref, rows, parts, ids, loss, gh, in_sem, out_sem):
    count, chunks = ids.shape[1], out_sem.shape[0] - 2
    chunk = out_ref.shape[0] // chunks
    pairs = ((ids_in, ids), (back_in, parts), (gh_in, gh), (loss_in, loss))
    reads = [pltpu.make_async_copy(src, dst, in_sem.at[n]) for n, (src, dst) in enumerate(pairs)]
    for read in reads:
        read.start()
    writes = []

    def write(src, dst):
        copy = pltpu.make_async_copy(src, dst, out_sem.at[len(writes)])
        copy.start()
        writes.append(copy)

    reads[0].wait()
    reads[1].wait()
    both = jnp.concatenate(split(parts[...]), axis=0)
    for n in range(chunks):
        index = lax.broadcasted_iota(jnp.int32, (chunk, count), 0) + n * chunk
        chosen = (index == ids[...]).astype(jnp.bfloat16)
        part = pl.ds(n * chunk, chunk)
        rows[part] = jnp.dot(jnp.concatenate([chosen, chosen], axis=1), both, preferred_element_type=jnp.float32)
        write(rows.at[part], out_ref.at[part])
        if n == 0:
            reads[2].wait()
            write(gh, gh_ref)
            reads[3].wait()
            write(loss, loss_ref)
    for copy in writes:
        copy.wait()


def local(table, hidden, neg_ids, pos_ids, dloss):
    rows, width = hidden.shape
    scale = 3.0 / math.sqrt(width)
    peers = lax.axis_size("dp")
    near = lax.axis_size("table") // 4
    ids = neg_ids[0, 0]
    per = neg_ids.shape[3]
    count = peers * per
    halves, blocks, piece = peers // 2, 2 * near, 2 * per
    f32, bf16 = jnp.float32, jnp.bfloat16
    pairs = pltpu.SemaphoreType.DMA((2, peers))
    nears = pltpu.SemaphoreType.DMA((near,))
    slices = pltpu.SemaphoreType.DMA((near, 4))
    crews = pltpu.SemaphoreType.DMA((2, near))
    vmem = pl.BlockSpec(memory_space=pltpu.VMEM)
    flops = 18 * 4 * count * near * rows * width
    loss, grad_hidden, returned = pl.pallas_call(
        functools.partial(kernel, peers, near, scale),
        out_shape=(
            jax.ShapeDtypeStruct((1, rows), f32),
            jax.ShapeDtypeStruct((rows, width), f32),
            jax.ShapeDtypeStruct((peers, per, width), f32),
        ),
        in_specs=[pl.BlockSpec(memory_space=pltpu.SMEM)] + [vmem] * 3 + [pl.BlockSpec(memory_space=pl.ANY)],
        out_specs=(vmem,) * 3,
        scratch_shapes=[
            pltpu.VMEM((peers, per, width), f32),
            pltpu.VMEM((8, rows), f32),
            pltpu.VMEM((2, peers, per, width), f32),
            pltpu.VMEM((2, halves, width, piece), bf16),
            pltpu.VMEM((2, halves, width, piece), bf16),
            pltpu.VMEM((2, near, rows, width), f32),
            pltpu.VMEM((2, near, rows, width), bf16),
            pltpu.VMEM((2, near, rows, width), bf16),
            pltpu.VMEM((2, near, 8, rows), f32),
            pltpu.VMEM((max(2 * count * blocks * rows // width, table.shape[0]), width), f32),
            pltpu.VMEM((2, halves, 2, near, 8, rows), f32),
            pltpu.VMEM((blocks, 2 * blocks, rows), f32),
            pltpu.VMEM((blocks, max(8, blocks), rows), f32),
            pltpu.VMEM((2, 8, rows), f32),
            pltpu.VMEM((2, near, 8, rows), f32),
            pltpu.VMEM((2, peers, per, width), f32),
            pltpu.VMEM((2, peers, per, width), f32),
            pltpu.VMEM((2, near, width, rows), f32),
            pltpu.VMEM((near, width, rows), f32),
            pltpu.VMEM((near, width, rows), f32),
            pltpu.SemaphoreType.DMA, pairs, pairs, slices, slices, slices, slices, nears, nears, nears, nears,
            crews, crews, crews, crews, pltpu.SemaphoreType.DMA, pltpu.SemaphoreType.DMA,
            pairs, pairs, nears, nears, slices, slices,
        ],
        compiler_params=pltpu.CompilerParams(
            collective_id=0, has_side_effects=True, vmem_limit_bytes=67043328
        ),
        cost_estimate=pl.CostEstimate(flops=flops, bytes_accessed=4 * count * width, transcendentals=0),
    )(ids, pos_ids.reshape(1, rows), dloss.reshape(1, rows), hidden, table)
    items = table.shape[0]
    chunks = items // math.gcd(512, items)
    anywhere = pl.BlockSpec(memory_space=pl.ANY)
    loss, grad_hidden, grad_table = pl.pallas_call(
        scatter,
        out_shape=(
            jax.ShapeDtypeStruct((1, rows), f32),
            jax.ShapeDtypeStruct((rows, width), f32),
            jax.ShapeDtypeStruct(table.shape, f32),
        ),
        in_specs=[anywhere] * 4,
        out_specs=(anywhere,) * 3,
        scratch_shapes=[
            pltpu.VMEM(table.shape, f32),
            pltpu.VMEM((count, width), f32),
            pltpu.VMEM((1, count), jnp.int32),
            pltpu.VMEM((1, rows), f32),
            pltpu.VMEM((rows, width), f32),
            pltpu.SemaphoreType.DMA((4,)),
            pltpu.SemaphoreType.DMA((chunks + 2,)),
        ],
        compiler_params=pltpu.CompilerParams(vmem_limit_bytes=67043328),
        cost_estimate=pl.CostEstimate(
            flops=4 * items * count * width, bytes_accessed=4 * items * width, transcendentals=0
        ),
    )(ids.reshape(1, count), loss, grad_hidden, returned.reshape(count, width))
    return (loss.reshape(rows), grad_hidden, grad_table)


def solution(mesh):
    in_specs = (
        P(("dp", "table"), None),
        P(("dp", "table"), None),
        P("dp", "table", None, None),
        P(("dp", "table")),
        P(("dp", "table")),
    )
    out_specs = (P(("dp", "table")), P(("dp", "table"), None), P(("dp", "table"), None))
    return jax.shard_map(local, mesh=mesh, in_specs=in_specs, out_specs=out_specs, check_vma=False)
```

```python
import functools
import math

import jax
import jax.numpy as jnp
from jax import lax
from jax.experimental import pallas as pl
from jax.experimental.pallas import tpu as pltpu
from jax.sharding import PartitionSpec as P

MESH = pl.DeviceIdType.MESH


def split(x):
    high = x.astype(jnp.bfloat16)
    return high, (x - high.astype(jnp.float32)).astype(jnp.bfloat16)


def kernel(
    peers, near, scale,
    ids_ref, pos_ref, dloss_ref, hid_ref, table_ref,
    loss_ref, gh_ref, back_ref,
    out, note, cand, ct_hi, ct_lo, hid, h_hi, h_lo, side, expo, bstat, stat, aim, lossbuf, merged, cg, ret, ght, ghmate, ghrecv,
    table_sem, c_send, c_recv, h_send, h_recv, m_send, m_recv, d_send, d_recv, e_send, e_recv,
    t_send, t_recv, a_send, a_recv, l_send, l_recv, z_send, z_recv, x_send, x_recv, g_send, g_recv,
):
    me = lax.axis_index("dp")
    t = lax.axis_index("table")
    a, k = me // 2, lax.rem(me, 2)
    hi, lo, s = t // (near * 2), lax.rem(t // 2, near), lax.rem(t, 2)
    rows, width = hid_ref.shape
    per = ids_ref.shape[1]
    halves = peers // 2
    count = peers * per
    piece = 2 * per
    blocks = 2 * near
    slices = h_send.shape[1]
    mine = a * 2 + s
    same = s == k
    other = 1 - k
    ln2 = math.log(2.0)
    bend = scale / ln2

    def place(far, mid, last):
        return far * (near * 2) + mid * 2 + last

    def wrap(base, step, size):
        return lax.rem(base + step, size)

    def device(da, dk, dh, dl, ds):
        return (
            wrap(a, da, halves) * 2 + wrap(k, dk, 2),
            place(wrap(hi, dh, 2), wrap(lo, dl, near), wrap(s, ds, 2)),
        )

    items = table_ref.shape[0]
    bring = pltpu.make_async_copy(table_ref, expo.at[pl.ds(0, items)], table_sem)
    bring.start()
    both = (0, 1)
    greet = [
        (da, dk, dh, dl, ds)
        for da in range(halves) for dk in both for dh in both for dl in range(near) for ds in both
        if (da, dk, dh, dl, ds) != (0, 0, 0, 0, 0) and (dl == 0 or (da == 0 and dh == 0))
    ]
    barrier = pltpu.get_barrier_semaphore()
    for g in greet:
        pl.semaphore_signal(barrier, inc=1, device_id=device(*g), device_id_type=MESH)
    note[0:1, :] = pos_ref[...].astype(jnp.float32)
    note[1:2, :] = dloss_ref[...]
    bring.wait()

    def pick(da, dc):
        g = wrap(a, da, halves) * 2 + wrap(s, dc, 2)

        def row(i, carry):
            out[g, pl.ds(i, 1), :] = expo[pl.ds(ids_ref[g, i], 1), :]
            return carry

        lax.fori_loop(0, per, row, 0, unroll=8)

    for da in range(halves - 1, -1, -1):
        for dc in both:
            pick(da, dc)
    pl.semaphore_wait(barrier, len(greet))

    started = []

    def send(src, dst, ssem, rsem, dev, own=None):
        copy = pltpu.make_async_remote_copy(
            src_ref=src, dst_ref=dst, send_sem=ssem, recv_sem=rsem, device_id=dev, device_id_type=MESH
        )
        if own is None:
            copy.start()
        else:
            @pl.when(own)
            def _():
                pltpu.make_async_copy(src, dst, rsem).start()

            @pl.when(jnp.logical_not(own))
            def _():
                copy.start()
        started.append((copy, own))

    def arrive(dst, rsem):
        pltpu.make_async_copy(dst, dst, rsem).wait()

    def send_cand(dh, da, dc):
        to = wrap(a, da, halves)
        g = to * 2 + wrap(s, dc, 2)
        send(
            out.at[g], cand.at[dh, me], c_send.at[dh, g], c_recv.at[dh, me],
            (to * 2 + s, place(wrap(hi, dh, 2), lo, wrap(s, dc, 2))),
            same if (dh, da, dc) == (0, 0, 0) else None,
        )

    parts_h = [pl.ds(q * (rows // slices), rows // slices) for q in range(slices)]

    def send_hid(dl):
        dev = (mine, place(hi, lo, k))
        send(note, side.at[s, lo], d_send.at[dl], d_recv.at[lo], dev, same)
        for q, part in enumerate(parts_h):
            send(hid_ref.at[part], hid.at[s, lo, part], h_send.at[dl, q], h_recv.at[lo, q], dev, same)

    later = range(1, near)
    far = range(halves - 1, -1, -1)
    send_hid(0)
    for da in far:
        send_cand(1, da, 0)
    for da in range(halves):
        send_cand(0, da, 0)
    send_cand(1, far[0], 1)

    mate = (a * 2 + other, t)

    def take_hid(dl):
        mid = wrap(lo, dl, near)
        arrive(side.at[k, mid], d_recv.at[mid])
        send(side.at[k, mid], side.at[k, mid], e_send.at[mid], e_recv.at[mid], mate)
        if dl == 0:
            for d in later:
                send(side.at[k, mid], side.at[k, mid], d_send.at[d], d_recv.at[mid], device(0, 0, 0, d, 0))
        for q, part in enumerate(parts_h):
            arrive(hid.at[k, mid, part], h_recv.at[mid, q])
            held = hid.at[k, mid, part]
            if dl == 0:
                for d in later:
                    send(held, held, h_send.at[d, q], h_recv.at[mid, q], device(0, 0, 0, d, 0))
            send(held, held, m_send.at[mid, q], m_recv.at[mid, q], mate)
        cut(k, mid)

    def take_mate(dl):
        mid = wrap(lo, dl, near)
        arrive(side.at[other, mid], e_recv.at[mid])
        for q, part in enumerate(parts_h):
            arrive(hid.at[other, mid, part], m_recv.at[mid, q])
        cut(other, mid)

    def cut(x, mid):
        top, low = split(hid[x, mid] * bend)
        h_hi[x, mid] = top
        h_lo[x, mid] = low

    def hits(dh, j, x, mid):
        base = place(wrap(hi, dh, 2), lo, k) * count + wrap(a, j, halves) * piece
        index = lax.broadcasted_iota(jnp.int32, (piece, rows), 0) + base
        return index == side[x, mid, 0:1, :].astype(jnp.int32)

    def take_cand(dh, j):
        for dk in both:
            source = wrap(a, j, halves) * 2 + wrap(k, dk, 2)
            arrive(cand.at[dh, source], c_recv.at[dh, source])

    folds = rows // width

    def slot(dh, j, x, mid, fold):
        first = ((((dh * halves + j) * 2 + x) * near + mid) * folds + fold) * piece
        return pl.ds(pl.multiple_of(first, piece), piece)

    def keep(dh, j, x, mid, value):
        for fold in range(folds):
            expo[slot(dh, j, x, mid, fold), :] = value[:, fold * width : (fold + 1) * width]

    def kept(dh, j, x, mid):
        return jnp.concatenate([expo[slot(dh, j, x, mid, fold), :] for fold in range(folds)], axis=1)

    def turn(dh, j):
        turned = split(cand[dh, pl.ds(wrap(a, j, halves) * 2, 2)].reshape(piece, width).T)
        ct_hi[dh, j] = turned[0]
        ct_lo[dh, j] = turned[1]

    def forward(dh, j, first, last):
        block = cand[dh, pl.ds(wrap(a, j, halves) * 2, 2)].reshape(piece, width)
        b_hi, b_lo = split(block)
        left = jnp.concatenate([b_hi, b_lo, b_hi], axis=1)

        def step(i, carry):
            x, mid = lax.rem(i, 2), wrap(lo, i // 2, near)
            right = jnp.concatenate([h_hi[x, mid], h_hi[x, mid], h_lo[x, mid]], axis=1)
            logits = lax.dot_general(
                left, right, (((1,), (1,)), ((), ())), preferred_element_type=jnp.float32
            )
            peak = jnp.max(logits, axis=0, keepdims=True)
            power = jnp.exp2(logits - peak)
            keep(dh, j, x, mid, power)
            bstat[dh, j, x, mid, 0:1, :] = peak
            bstat[dh, j, x, mid, 1:2, :] = jnp.sum(power, axis=0, keepdims=True)
            bstat[dh, j, x, mid, 2:3, :] = jnp.sum(
                jnp.where(hits(dh, j, x, mid), logits, 0.0), axis=0, keepdims=True
            )
            return carry

        lax.fori_loop(first, last, step, 0, unroll=2)

    STEPS = [(take_hid, 0), (take_mate, 0)]
    STEPS += [(send_cand, 0, da, 1) for da in range(halves)] + [(send_cand, 1, da, 1) for da in far[1:]]
    for j in range(halves):
        STEPS += [(take_cand, 0, j), (forward, 0, j, 0, 2), (turn, 0, j)]
    STEPS += [(take_cand, 1, far[0]), (forward, 1, far[0], 0, 2), (turn, 1, far[0])]
    STEPS += [(take_hid, dl) for dl in later] + [(take_mate, dl) for dl in later]
    STEPS += [(forward, 0, j, 2, blocks) for j in range(halves)]
    STEPS += [(forward, 1, far[0], 2, blocks)]
    for j in far[1:]:
        STEPS += [(take_cand, 1, j), (forward, 1, j, 0, blocks)]
    for todo in STEPS:
        todo[0](*todo[1:])

    parts = [(dh, j) for dh in both for j in range(halves)]
    seat = k * near + lo
    for x in both:
        for mid in range(near):
            m = x * near + mid
            peak = bstat[0, 0, x, mid, 0:1, :]
            for p in parts[1:]:
                peak = jnp.maximum(peak, bstat[p[0], p[1], x, mid, 0:1, :])
            total = jnp.zeros_like(peak)
            target = jnp.zeros_like(peak)
            for p in parts:
                total += bstat[p[0], p[1], x, mid, 1:2, :] * jnp.exp2(bstat[p[0], p[1], x, mid, 0:1, :] - peak)
                target += bstat[p[0], p[1], x, mid, 2:3, :]
            stat[seat, m : m + 1, :] = peak
            stat[seat, blocks + m : blocks + m + 1, :] = total
            aim[seat, m : m + 1, :] = target
    crew = [(dk, dl) for dl in range(near - 1, -1, -1) for dk in both if (dk, dl) != (0, 0)]
    for dk, dl in crew:
        send(
            stat.at[seat], stat.at[seat], t_send.at[dk, dl], t_recv.at[dk, dl], device(0, dk, 0, dl, 0)
        )
    for dk, dl in crew:
        send(
            aim.at[seat], aim.at[seat], a_send.at[dk, dl], a_recv.at[dk, dl], device(0, dk, 0, dl, 0)
        )
    for j in far[1:]:
        turn(1, j)
    for dk, dl in crew:
        came = wrap(k, dk, 2) * near + wrap(lo, near - dl, near)
        arrive(stat.at[came], t_recv.at[dk, dl])

    for x in both:
        for mid in range(near):
            m = x * near + mid
            peak = stat[0, m : m + 1, :]
            for w in range(1, blocks):
                peak = jnp.maximum(peak, stat[w, m : m + 1, :])
            total = jnp.zeros_like(peak)
            for w in range(blocks):
                total += stat[w, blocks + m : blocks + m + 1, :] * jnp.exp2(stat[w, m : m + 1, :] - peak)
            weight = ln2 * side[x, mid, 1:2, :]
            merged[x, mid, 0:1, :] = peak
            merged[x, mid, 1:2, :] = weight / total
            merged[x, mid, 2:3, :] = weight
            merged[x, mid, 3:4, :] = ln2 * peak + jnp.log(total)

    def backward(dh, j, first, last, fresh):
        flip = jnp.concatenate([ct_hi[dh, j], ct_hi[dh, j], ct_lo[dh, j]], axis=1)

        def step(i, acc):
            x, mid = lax.rem(i, 2), wrap(lo, i // 2, near)
            weight = merged[x, mid, 2:3, :]
            factor = merged[x, mid, 1:2, :] * jnp.exp2(bstat[dh, j, x, mid, 0:1, :] - merged[x, mid, 0:1, :])
            power = kept(dh, j, x, mid) * factor
            c_hi, c_lo = split(jnp.where(hits(dh, j, x, mid), power - weight, power))
            term = jnp.dot(
                flip, jnp.concatenate([c_hi, c_lo, c_hi], axis=0), preferred_element_type=jnp.float32
            )
            if fresh:
                ght[x, mid] = term
            else:
                ght[x, mid] += term
            return acc + jnp.dot(
                jnp.concatenate([c_hi, c_lo, c_hi], axis=1),
                jnp.concatenate([h_hi[x, mid], h_hi[x, mid], h_lo[x, mid]], axis=0),
                preferred_element_type=jnp.float32,
            )

        start = wrap(a, j, halves) * 2
        if last == blocks:
            acc = jnp.zeros((piece, width), jnp.float32)
        else:
            acc = cg[dh, pl.ds(start, 2)].reshape(piece, width)
        acc = lax.fori_loop(first, last, step, acc, unroll=4 if last - first == 4 else 2)
        cg[dh, pl.ds(start, 2)] = acc.reshape(2, per, width)

    def send_back(dh, j):
        start = wrap(a, j, halves) * 2
        for dk in both:
            source = start + wrap(k, dk, 2)
            send(
                cg.at[dh, source], ret.at[dh, mine], z_send.at[dh, source], z_recv.at[dh, mine],
                (source, place(wrap(hi, dh, 2), lo, k)),
                same if (dh, j, dk) == (0, 0, 0) else None,
            )

    slices = g_send.shape[1]
    parts_g = [pl.ds(q * (width // slices), width // slices) for q in range(slices)]

    def pass_hid(dl):
        mid = wrap(lo, dl, near)
        send(ght.at[other, mid], ghmate.at[mid], x_send.at[mid], x_recv.at[mid], mate)

    def sum_hid(dl):
        mid = wrap(lo, dl, near)
        arrive(ghmate.at[mid], x_recv.at[mid])
        ght[k, mid] += ghmate[mid]
        for q, part in enumerate(parts_g):
            send(
                ght.at[k, mid, part], ghrecv.at[lo, part], g_send.at[dl, q], g_recv.at[lo, q],
                (mine, place(hi, mid, k)), same if dl == 0 else None,
            )

    order = [(1, j) for j in far] + [(0, j) for j in far]
    head, tail = order[0], order[1:]
    STEPS = [(backward, *p, 2, blocks, p == head) for p in order]
    STEPS += [(pass_hid, dl) for dl in later]
    STEPS += [(backward, *head, 0, 2, 2), (send_back, *head)]
    STEPS += [(sum_hid, dl) for dl in later]
    for p in tail:
        STEPS += [(backward, *p, 0, 2, False), (send_back, *p)]
    STEPS += [(pass_hid, 0), (sum_hid, 0)]
    for todo in STEPS:
        todo[0](*todo[1:])

    for dk, dl in crew:
        came = wrap(k, dk, 2) * near + wrap(lo, near - dl, near)
        arrive(aim.at[came], a_recv.at[dk, dl])
    target = jnp.zeros((1, rows), jnp.float32)
    for w in range(blocks):
        target += aim[w, pl.ds(seat, 1), :]
    lossbuf[0] = jnp.broadcast_to(merged[k, lo, 3:4, :] - ln2 * target, lossbuf.shape[1:])
    send(lossbuf.at[0], lossbuf.at[1], l_send, l_recv, (mine, place(hi, lo, k)), same)

    for dl in range(near):
        mid = wrap(lo, dl, near)
        for q, part in enumerate(parts_g):
            arrive(ghrecv.at[mid, part], g_recv.at[mid, q])
    whole = ghrecv[0]
    for mid in range(1, near):
        whole += ghrecv[mid]
    gh_ref[...] = (bend * whole).T
    arrive(lossbuf.at[1], l_recv)
    loss_ref[...] = lossbuf[1, 0:1, :]
    for dh in both:
        for g in range(peers):
            arrive(ret.at[dh, g], z_recv.at[dh, g])
    back_ref[...] = ret[0] + ret[1]
    for copy, own in started:
        if own is None:
            copy.wait_send()
        else:
            @pl.when(jnp.logical_not(own))
            def _():
                copy.wait_send()


def scatter(ids_in, loss_in, gh_in, back_in, loss_ref, gh_ref, out_ref, rows, parts, ids, loss, gh, in_sem, out_sem):
    count, chunks = ids.shape[1], out_sem.shape[0] - 2
    chunk = out_ref.shape[0] // chunks
    pairs = ((ids_in, ids), (back_in, parts), (gh_in, gh), (loss_in, loss))
    reads = [pltpu.make_async_copy(src, dst, in_sem.at[n]) for n, (src, dst) in enumerate(pairs)]
    for read in reads:
        read.start()
    writes = []

    def write(src, dst):
        copy = pltpu.make_async_copy(src, dst, out_sem.at[len(writes)])
        copy.start()
        writes.append(copy)

    reads[0].wait()
    reads[1].wait()
    both = jnp.concatenate(split(parts[...]), axis=0)
    for n in range(chunks):
        index = lax.broadcasted_iota(jnp.int32, (chunk, count), 0) + n * chunk
        chosen = (index == ids[...]).astype(jnp.bfloat16)
        part = pl.ds(n * chunk, chunk)
        rows[part] = jnp.dot(jnp.concatenate([chosen, chosen], axis=1), both, preferred_element_type=jnp.float32)
        write(rows.at[part], out_ref.at[part])
        if n == 0:
            reads[2].wait()
            write(gh, gh_ref)
            reads[3].wait()
            write(loss, loss_ref)
    for copy in writes:
        copy.wait()


def local(table, hidden, neg_ids, pos_ids, dloss):
    rows, width = hidden.shape
    scale = 3.0 / math.sqrt(width)
    peers = lax.axis_size("dp")
    near = lax.axis_size("table") // 4
    ids = neg_ids[0, 0]
    per = neg_ids.shape[3]
    count = peers * per
    halves, blocks, piece = peers // 2, 2 * near, 2 * per
    f32, bf16 = jnp.float32, jnp.bfloat16
    pairs = pltpu.SemaphoreType.DMA((2, peers))
    nears = pltpu.SemaphoreType.DMA((near,))
    slices = pltpu.SemaphoreType.DMA((near, 4))
    crews = pltpu.SemaphoreType.DMA((2, near))
    vmem = pl.BlockSpec(memory_space=pltpu.VMEM)
    flops = 18 * 4 * count * near * rows * width
    loss, grad_hidden, returned = pl.pallas_call(
        functools.partial(kernel, peers, near, scale),
        out_shape=(
            jax.ShapeDtypeStruct((1, rows), f32),
            jax.ShapeDtypeStruct((rows, width), f32),
            jax.ShapeDtypeStruct((peers, per, width), f32),
        ),
        in_specs=[pl.BlockSpec(memory_space=pltpu.SMEM)] + [vmem] * 3 + [pl.BlockSpec(memory_space=pl.ANY)],
        out_specs=(vmem,) * 3,
        scratch_shapes=[
            pltpu.VMEM((peers, per, width), f32),
            pltpu.VMEM((8, rows), f32),
            pltpu.VMEM((2, peers, per, width), f32),
            pltpu.VMEM((2, halves, width, piece), bf16),
            pltpu.VMEM((2, halves, width, piece), bf16),
            pltpu.VMEM((2, near, rows, width), f32),
            pltpu.VMEM((2, near, rows, width), bf16),
            pltpu.VMEM((2, near, rows, width), bf16),
            pltpu.VMEM((2, near, 8, rows), f32),
            pltpu.VMEM((max(2 * count * blocks * rows // width, table.shape[0]), width), f32),
            pltpu.VMEM((2, halves, 2, near, 8, rows), f32),
            pltpu.VMEM((blocks, 2 * blocks, rows), f32),
            pltpu.VMEM((blocks, max(8, blocks), rows), f32),
            pltpu.VMEM((2, 8, rows), f32),
            pltpu.VMEM((2, near, 8, rows), f32),
            pltpu.VMEM((2, peers, per, width), f32),
            pltpu.VMEM((2, peers, per, width), f32),
            pltpu.VMEM((2, near, width, rows), f32),
            pltpu.VMEM((near, width, rows), f32),
            pltpu.VMEM((near, width, rows), f32),
            pltpu.SemaphoreType.DMA, pairs, pairs, slices, slices, slices, slices, nears, nears, nears, nears,
            crews, crews, crews, crews, pltpu.SemaphoreType.DMA, pltpu.SemaphoreType.DMA,
            pairs, pairs, nears, nears, slices, slices,
        ],
        compiler_params=pltpu.CompilerParams(
            collective_id=0, has_side_effects=True, vmem_limit_bytes=67043328
        ),
        cost_estimate=pl.CostEstimate(flops=flops, bytes_accessed=4 * count * width, transcendentals=0),
    )(ids, pos_ids.reshape(1, rows), dloss.reshape(1, rows), hidden, table)
    items = table.shape[0]
    chunks = items // math.gcd(256, items)
    anywhere = pl.BlockSpec(memory_space=pl.ANY)
    loss, grad_hidden, grad_table = pl.pallas_call(
        scatter,
        out_shape=(
            jax.ShapeDtypeStruct((1, rows), f32),
            jax.ShapeDtypeStruct((rows, width), f32),
            jax.ShapeDtypeStruct(table.shape, f32),
        ),
        in_specs=[anywhere] * 4,
        out_specs=(anywhere,) * 3,
        scratch_shapes=[
            pltpu.VMEM(table.shape, f32),
            pltpu.VMEM((count, width), f32),
            pltpu.VMEM((1, count), jnp.int32),
            pltpu.VMEM((1, rows), f32),
            pltpu.VMEM((rows, width), f32),
            pltpu.SemaphoreType.DMA((4,)),
            pltpu.SemaphoreType.DMA((chunks + 2,)),
        ],
        compiler_params=pltpu.CompilerParams(vmem_limit_bytes=67043328),
        cost_estimate=pl.CostEstimate(
            flops=4 * items * count * width, bytes_accessed=4 * items * width, transcendentals=0
        ),
    )(ids.reshape(1, count), loss, grad_hidden, returned.reshape(count, width))
    return (loss.reshape(rows), grad_hidden, grad_table)


def solution(mesh):
    in_specs = (
        P(("dp", "table"), None),
        P(("dp", "table"), None),
        P("dp", "table", None, None),
        P(("dp", "table")),
        P(("dp", "table")),
    )
    out_specs = (P(("dp", "table")), P(("dp", "table"), None), P(("dp", "table"), None))
    return jax.shard_map(local, mesh=mesh, in_specs=in_specs, out_specs=out_specs, check_vma=False)
```
